256 devices in a mesh: row: 8 (over z), col: 32 (over y, x, core).
Axes of the slice: x: 4, y: 4, z: 8, core: 2. Of those that a mesh axis runs over, the one named last changes fastest.
Arguments:
- factor_tiles: bfloat16 [3, 96, 64, 2048], P(None, 'row', None, 'col'), may hold values from -0.3125 to 0.3125
- tile_row: int32 [3, 96, 32], P(None, 'row', 'col'), may hold values from 0 to 63
- tile_col: int32 [3, 96, 32], P(None, 'row', 'col'), may hold values from 0 to 15
- right_sides: float32 [4, 512, 64, 128], P(None, ('col', 'row')), may hold values from -6 to 6
- diag_inverse: float32 [4, 64, 32768], P(None, None, ('col', 'row')), as said below
Outputs:
- preconditioned: float32 [4, 512, 64, 128], P(None, ('col', 'row'))
The draws below stay inside these ranges and needn't reach their ends.
Inputs may be any that keep to these rules, and one draw needn't show every extreme that they name: `tile_row`: a block row within its row group. `tile_col`: a block column within its column group. `diag_inverse`: diagonal entries of every block between 0.5 and 2.
All inputs are finite; a program needn't handle non-finite values.
Results may differ from the reference program's by a relative error of at most 0.025.
Values may be sent and summed in bfloat16 or wider, within the bound.
A program may use at most 64 MiB of HBM per device.

```python
import math
import jax
import jax.numpy as jnp
from jax import lax

BLOCK = 64
VECTORS = 128
ROWS_DEV = 2
TILE_SHARE = 6
LEVELS = 3
LEVEL_ROWS = 512
GROUP_ROWS = 16
LOCAL_ROWS = 64
TILES_DEV = 12
N_ROW = 8
N_COL = 32


def draw_diag_inverse(key, part):
    first_key, second_key = jax.random.split(key)
    shape = (LEVELS + 1, BLOCK, LEVEL_ROWS * BLOCK)
    noise = jax.random.normal(first_key, shape, jnp.float32)
    noise = noise * (0.4 / math.sqrt(BLOCK))
    diagonal = jnp.exp(jax.random.uniform(second_key, shape, jnp.float32, math.log(0.5), math.log(2.0)))
    column_pos = jnp.arange(shape[1], dtype=jnp.int32)[None, :, None]
    row_pos = jnp.arange(shape[2], dtype=jnp.int32)[None, None, :] % BLOCK
    return jnp.where(column_pos == row_pos, diagonal, noise)


def set_ends(entries, stream_key, least, high):
    place = [jax.random.randint(jax.random.fold_in(stream_key, axis), (), 0, length) for axis, length in enumerate(entries.shape)]
    longest = entries.shape.index(max(entries.shape))
    neighbour = place[:longest] + [(place[longest] + 1) % entries.shape[longest]] + place[longest + 1:]
    return entries.at[tuple(place)].set(least).at[tuple(neighbour)].set(high)


def block_scale(key, shape, cuts, smallest, largest):
    def one(axis_at, parts):
        steps = jax.random.uniform(jax.random.fold_in(jax.random.fold_in(key, 6), axis_at), (parts,), jnp.float32, smallest / len(cuts), largest / len(cuts))
        return jnp.repeat(jnp.exp(steps), shape[axis_at] // parts).reshape((-1,) + (1,) * (len(shape) - axis_at - 1))

    factor_of = one(*cuts[0])
    for cut in cuts[1:]:
        factor_of = factor_of * one(*cut)
    return factor_of


def normal_values(stream_key, shape, scale, most, cuts=(), kind=jnp.bfloat16):
    drawn = scale * jax.random.normal(stream_key, shape, jnp.float32)
    if cuts:
        drawn = drawn * block_scale(stream_key, shape, cuts, -0.22, 0.18)
    return jnp.clip(drawn, -most, most).astype(kind)


def setup_inputs(seed: int = 0) -> dict:
    seeds = jax.random.split(jax.random.key(seed), 6)
    return {
        "factor_tiles": normal_values(seeds[0], (LEVELS, N_ROW * TILES_DEV, BLOCK, N_COL * BLOCK), (TILE_SHARE * BLOCK) ** -0.5, 0.3125, ((1, 8), (3, 32))),
        "tile_row": set_ends(jax.random.randint(seeds[1], (LEVELS, N_ROW * TILES_DEV, N_COL), 0, LOCAL_ROWS), jax.random.fold_in(seeds[1], 1), 0, LOCAL_ROWS - 1).astype(jnp.int32),
        "tile_col": set_ends(jax.random.randint(seeds[2], (LEVELS, N_ROW * TILES_DEV, N_COL), 0, GROUP_ROWS), jax.random.fold_in(seeds[2], 1), 0, GROUP_ROWS - 1).astype(jnp.int32),
        "right_sides": normal_values(seeds[3], (LEVELS + 1, LEVEL_ROWS, BLOCK, VECTORS), 1.0, 6.0, ((1, 256),), jnp.float32),
        "diag_inverse": draw_diag_inverse(jax.random.fold_in(seeds[5], 71), 0),
    }


def apply_inverse(inverse, vector, transposed):
    matrix = inverse.reshape(inverse.shape[0], -1, inverse.shape[0])
    if transposed:
        return jnp.einsum("cir,irn->icn", matrix, vector, precision=lax.Precision.HIGHEST)
    return jnp.einsum("cir,icn->irn", matrix, vector, precision=lax.Precision.HIGHEST)


def rounded(value):
    return lax.optimization_barrier(value.astype(jnp.bfloat16)).astype(jnp.float32)


def reference(factor_tiles, tile_row, tile_col, right_sides, diag_inverse):
    tile_all = factor_tiles.reshape(LEVELS, N_ROW * TILES_DEV, BLOCK, N_COL, BLOCK).transpose(0, 1, 3, 2, 4)
    owner_group = (jnp.arange(N_ROW * TILES_DEV, dtype=jnp.int32) // TILES_DEV)[None, :, None]
    local_q = tile_row.astype(jnp.int32)
    global_rows = ((local_q // ROWS_DEV) * N_ROW + owner_group) * ROWS_DEV + local_q % ROWS_DEV
    global_cols = jnp.arange(N_COL, dtype=jnp.int32)[None, None, :] * GROUP_ROWS + tile_col.astype(jnp.int32)
    solved = [apply_inverse(diag_inverse[0], right_sides[0], False)]
    for section_no in range(1, LEVELS + 1):
        earlier = solved[-1].astype(jnp.bfloat16)

        def group_term(total, inputs, earlier=earlier):
            tile_block, row_block, col_block = inputs
            picked = earlier[col_block].astype(jnp.float32)
            product = jnp.einsum("tab,tbn->tan", tile_block.astype(jnp.float32), picked,
                                 precision=lax.Precision.HIGHEST)
            part = jax.ops.segment_sum(product, row_block, num_segments=LEVEL_ROWS)
            return total + rounded(part), None

        inputs = (tile_all[section_no - 1].transpose(1, 0, 2, 3),
                  global_rows[section_no - 1].T, global_cols[section_no - 1].T)
        initial = jnp.zeros((LEVEL_ROWS, BLOCK, VECTORS), jnp.float32)
        coupled, unused = lax.scan(group_term, initial, inputs)
        solved.append(apply_inverse(diag_inverse[section_no], right_sides[section_no] - coupled, False))
    result = [None] * (LEVELS + 1)
    result[LEVELS] = apply_inverse(diag_inverse[LEVELS], solved[LEVELS], True)
    for section_no in range(LEVELS - 1, -1, -1):
        upper = result[section_no + 1].astype(jnp.bfloat16)

        def row_term(total, inputs, upper=upper):
            tile_block, row_block, col_block = inputs
            picked = upper[row_block].astype(jnp.float32)
            spread = jnp.einsum("tab,tan->tbn", tile_block.astype(jnp.float32), picked,
                                precision=lax.Precision.HIGHEST)
            part = jax.ops.segment_sum(spread, col_block, num_segments=LEVEL_ROWS)
            return total + rounded(part), None

        inputs = (tile_all[section_no].reshape(N_ROW, TILES_DEV * N_COL, BLOCK, BLOCK),
                  global_rows[section_no].reshape(N_ROW, TILES_DEV * N_COL),
                  global_cols[section_no].reshape(N_ROW, TILES_DEV * N_COL))
        initial = jnp.zeros((LEVEL_ROWS, BLOCK, VECTORS), jnp.float32)
        back, unused = lax.scan(row_term, initial, inputs)
        result[section_no] = apply_inverse(diag_inverse[section_no], solved[section_no] - back, True)
    return jnp.stack(result)
```

```python
import functools

import jax
import jax.numpy as jnp
from jax import lax
from jax.experimental import pallas as pl
from jax.experimental.pallas import tpu as pltpu
from jax.sharding import PartitionSpec as P

MESH = pl.DeviceIdType.MESH
AXES = ("row", "col")


def apply_inverse(inverse, vector, transposed):
    matrix = inverse.reshape(inverse.shape[0], -1, inverse.shape[0])
    if transposed:
        return jnp.einsum("cir,irn->icn", matrix, vector, precision=lax.Precision.HIGHEST)
    return jnp.einsum("cir,icn->irn", matrix, vector, precision=lax.Precision.HIGHEST)


def peer_id(axis, peer):
    return tuple(peer if name == axis else lax.axis_index(name) for name in AXES)


def greet(axis, n, me):
    barrier = pltpu.get_barrier_semaphore()
    for k in range(1, n):
        pl.semaphore_signal(
            barrier, inc=1, device_id=peer_id(axis, lax.rem(me + k, n)), device_id_type=MESH
        )
    pl.semaphore_wait(barrier, n - 1)


def exchange_sum_kernel(axis, n, x_ref, o_ref, held, send_sem, recv_sem):
    me = lax.axis_index(axis)
    greet(axis, n, me)
    copies = []
    for k in range(1, n):
        peer = lax.rem(me + k, n)
        copy = pltpu.make_async_remote_copy(
            src_ref=x_ref.at[peer],
            dst_ref=held.at[k],
            send_sem=send_sem.at[k],
            recv_sem=recv_sem.at[k],
            device_id=peer_id(axis, peer),
            device_id_type=MESH,
        )
        copy.start()
        copies.append(copy)
    total = x_ref[me].astype(jnp.float32)
    for k in range(1, n):
        copies[k - 1].wait()
        total = total + held[k].astype(jnp.float32)
    o_ref[...] = total


def gather_kernel(axis, n, x_ref, o_ref, held, send_sem, recv_sem):
    me = lax.axis_index(axis)
    greet(axis, n, me)
    copies = []
    for k in range(1, n):
        peer = lax.rem(me + k, n)
        copy = pltpu.make_async_remote_copy(
            src_ref=x_ref,
            dst_ref=held.at[k],
            send_sem=send_sem.at[k],
            recv_sem=recv_sem.at[k],
            device_id=peer_id(axis, peer),
            device_id_type=MESH,
        )
        copy.start()
        copies.append(copy)
    o_ref[me] = x_ref[...]
    for k in range(1, n):
        copies[k - 1].wait()
        o_ref[lax.rem(me + n - k, n)] = held[k]


def exchange_sum(x, axis, n, cid):
    piece = x.shape[1:]
    return pl.pallas_call(
        functools.partial(exchange_sum_kernel, axis, n),
        out_shape=jax.ShapeDtypeStruct(piece, jnp.float32),
        in_specs=[pl.BlockSpec(memory_space=pltpu.VMEM)],
        out_specs=pl.BlockSpec(memory_space=pltpu.VMEM),
        scratch_shapes=[
            pltpu.VMEM((n,) + piece, x.dtype),
            pltpu.SemaphoreType.DMA((n,)),
            pltpu.SemaphoreType.DMA((n,)),
        ],
        compiler_params=pltpu.CompilerParams(collective_id=cid, has_side_effects=True),
    )(x)


def gather(x, axis, n, cid):
    return pl.pallas_call(
        functools.partial(gather_kernel, axis, n),
        out_shape=jax.ShapeDtypeStruct((n,) + x.shape, x.dtype),
        in_specs=[pl.BlockSpec(memory_space=pltpu.VMEM)],
        out_specs=pl.BlockSpec(memory_space=pltpu.VMEM),
        scratch_shapes=[
            pltpu.VMEM((n,) + x.shape, x.dtype),
            pltpu.SemaphoreType.DMA((n,)),
            pltpu.SemaphoreType.DMA((n,)),
        ],
        compiler_params=pltpu.CompilerParams(collective_id=cid, has_side_effects=True),
    )(x)


def solve_all(n_row, n_col, factor_tiles, tile_row, tile_col, right_sides, diag_inverse):
    levels = factor_tiles.shape[0]
    rows_dev = right_sides.shape[1]
    group_rows = rows_dev * n_row
    row_ids = tile_row[:, :, 0]
    col_ids = tile_col[:, :, 0]
    current = apply_inverse(diag_inverse[0], right_sides[0], False)
    solved = [current]
    for section_no in range(1, levels + 1):
        gathered = gather(current.astype(jnp.bfloat16), "row", n_row, 1)
        gathered = gathered.reshape((group_rows,) + current.shape[1:])
        picked = gathered[col_ids[section_no - 1]]
        products = jnp.einsum(
            "tab,tbn->tan", factor_tiles[section_no - 1], picked, preferred_element_type=jnp.float32
        )
        targets = row_ids[section_no - 1]
        places = jnp.arange(n_col * rows_dev, dtype=jnp.int32)
        select = (targets[:, None] == places[None, :]).astype(jnp.float32)
        terms = jnp.einsum("tq,tan->qan", select, products, precision=lax.Precision.HIGHEST)
        terms = terms.astype(jnp.bfloat16).reshape((n_col, rows_dev) + terms.shape[1:])
        row_sums = exchange_sum(terms, "col", n_col, 2)
        current = apply_inverse(diag_inverse[section_no], right_sides[section_no] - row_sums, False)
        solved.append(current)
    current = apply_inverse(diag_inverse[levels], solved[levels], True)
    result = [current]
    columns_here = jnp.arange(group_rows, dtype=jnp.int32)
    for section_no in range(levels - 1, -1, -1):
        everyone = gather(current.astype(jnp.bfloat16), "col", n_col, 3)
        everyone = everyone.reshape((n_col * rows_dev,) + current.shape[1:])
        picked = everyone[row_ids[section_no]]
        spread = jnp.einsum(
            "tab,tan->tbn", factor_tiles[section_no], picked, preferred_element_type=jnp.float32
        )
        select = (col_ids[section_no][:, None] == columns_here[None, :]).astype(jnp.float32)
        column_sums = jnp.einsum("tj,tbn->jbn", select, spread, precision=lax.Precision.HIGHEST)
        column_sums = column_sums.astype(jnp.bfloat16).reshape((n_row, rows_dev) + column_sums.shape[1:])
        received = exchange_sum(column_sums, "row", n_row, 4)
        current = apply_inverse(diag_inverse[section_no], solved[section_no] - received, True)
        result.insert(0, current)
    return jnp.stack(result)


def solution(mesh):
    n_row, n_col = mesh.shape["row"], mesh.shape["col"]
    return jax.shard_map(
        functools.partial(solve_all, n_row, n_col),
        mesh=mesh,
        in_specs=(
            P(None, "row", None, "col"),
            P(None, "row", "col"),
            P(None, "row", "col"),
            P(None, ("col", "row"), None, None),
            P(None, None, ("col", "row")),
        ),
        out_specs=P(None, ("col", "row"), None, None),
        check_vma=False,
    )
```

```python
import functools

import jax
import jax.numpy as jnp
from jax import lax
from jax.experimental import pallas as pl
from jax.experimental.pallas import tpu as pltpu
from jax.sharding import PartitionSpec as P

MESH = pl.DeviceIdType.MESH
AXES = ("row", "col")
HIGHEST = lax.Precision.HIGHEST


def peer_id(axis, peer):
    return tuple(peer if name == axis else lax.axis_index(name) for name in AXES)


def level_kernel(ex, ga, applies, *refs):
    refs = list(refs)
    x_ref = refs.pop(0) if ex else None
    base_ref = refs.pop(0)
    g_refs = [refs.pop(0) for _ in applies]
    out_ref = refs.pop(0)
    gathered_ref = refs.pop(0) if ga else None
    if ex:
        held_x, ex_send, ex_recv = refs.pop(0), refs.pop(0), refs.pop(0)
    if ga:
        held_g, stage, ga_send, ga_recv = refs.pop(0), refs.pop(0), refs.pop(0), refs.pop(0)

    groups = [g for g in (ex, ga) if g]
    barrier = pltpu.get_barrier_semaphore()
    for axis, n in groups:
        me = lax.axis_index(axis)
        for k in range(1, n):
            pl.semaphore_signal(
                barrier, inc=1, device_id=peer_id(axis, lax.rem(me + k, n)), device_id_type=MESH
            )
    pl.semaphore_wait(barrier, sum(n - 1 for _, n in groups))

    value = base_ref[...]
    if ex:
        axis, n = ex
        me = lax.axis_index(axis)
        copies = []
        for k in range(1, n):
            peer = lax.rem(me + k, n)
            copy = pltpu.make_async_remote_copy(
                src_ref=x_ref.at[peer],
                dst_ref=held_x.at[k],
                send_sem=ex_send.at[k],
                recv_sem=ex_recv.at[k],
                device_id=peer_id(axis, peer),
                device_id_type=MESH,
            )
            copy.start()
            copies.append(copy)
        total = x_ref[me].astype(jnp.float32)
        for k in range(1, n):
            copies[k - 1].wait()
            total = total + held_x[k].astype(jnp.float32)
        value = value - total
    for g_ref in g_refs:
        value = jnp.stack(
            [
                jnp.dot(g_ref[i], value[i], precision=HIGHEST, preferred_element_type=jnp.float32)
                for i in range(value.shape[0])
            ]
        )
    out_ref[...] = value
    if ga:
        axis, n = ga
        me = lax.axis_index(axis)
        stage[...] = value.astype(stage.dtype)
        copies = []
        for k in range(1, n):
            peer = lax.rem(me + k, n)
            copy = pltpu.make_async_remote_copy(
                src_ref=stage,
                dst_ref=held_g.at[k],
                send_sem=ga_send.at[k],
                recv_sem=ga_recv.at[k],
                device_id=peer_id(axis, peer),
                device_id_type=MESH,
            )
            copy.start()
            copies.append(copy)
        gathered_ref[me] = value.astype(gathered_ref.dtype)
        for k in range(1, n):
            copies[k - 1].wait()
            gathered_ref[lax.rem(me + n - k, n)] = held_g[k]


def level(cid, x, base, gs, ex=None, ga=None):
    piece = base.shape
    vmem = pl.BlockSpec(memory_space=pltpu.VMEM)
    args = ([x] if ex else []) + [base] + list(gs)
    out_shape = [jax.ShapeDtypeStruct(piece, jnp.float32)]
    scratch = []
    if ex:
        scratch += [
            pltpu.VMEM((ex[1],) + piece, jnp.bfloat16),
            pltpu.SemaphoreType.DMA((ex[1],)),
            pltpu.SemaphoreType.DMA((ex[1],)),
        ]
    if ga:
        out_shape.append(jax.ShapeDtypeStruct((ga[1],) + piece, jnp.bfloat16))
        scratch += [
            pltpu.VMEM((ga[1],) + piece, jnp.bfloat16),
            pltpu.VMEM(piece, jnp.bfloat16),
            pltpu.SemaphoreType.DMA((ga[1],)),
            pltpu.SemaphoreType.DMA((ga[1],)),
        ]
    outs = pl.pallas_call(
        functools.partial(level_kernel, ex, ga, tuple(range(len(gs)))),
        out_shape=out_shape,
        in_specs=[vmem] * len(args),
        out_specs=[vmem] * len(out_shape),
        scratch_shapes=scratch,
        compiler_params=pltpu.CompilerParams(collective_id=cid, has_side_effects=True),
    )(*args)
    return outs if ga else (outs[0], None)


def solve_all(n_row, n_col, factor_tiles, tile_row, tile_col, right_sides, diag_inverse):
    levels = factor_tiles.shape[0]
    rows_dev = right_sides.shape[1]
    block = right_sides.shape[2]
    group_rows = rows_dev * n_row
    row_ids = tile_row[:, :, 0]
    col_ids = tile_col[:, :, 0]
    split = diag_inverse.reshape(levels + 1, block, rows_dev, block)
    g_fwd = split.transpose(0, 2, 3, 1)
    g_bwd = split.transpose(0, 2, 1, 3)
    row_axis, col_axis = ("row", n_row), ("col", n_col)

    current, gathered = level(1, None, right_sides[0], [g_fwd[0]], ga=row_axis)
    solved = [current]
    for section_no in range(1, levels + 1):
        picked = gathered.reshape((group_rows,) + current.shape[1:])[col_ids[section_no - 1]]
        products = jnp.einsum(
            "tab,tbn->tan", factor_tiles[section_no - 1], picked, preferred_element_type=jnp.float32
        )
        targets = row_ids[section_no - 1]
        places = jnp.arange(n_col * rows_dev, dtype=jnp.int32)
        select = (targets[:, None] == places[None, :]).astype(jnp.float32)
        terms = jnp.einsum("tq,tan->qan", select, products, precision=HIGHEST)
        terms = terms.astype(jnp.bfloat16).reshape((n_col, rows_dev) + terms.shape[1:])
        if section_no < levels:
            current, gathered = level(2, terms, right_sides[section_no], [g_fwd[section_no]],
                                      ex=col_axis, ga=row_axis)
            solved.append(current)
        else:
            current, gathered = level(3, terms, right_sides[section_no],
                                      [g_fwd[section_no], g_bwd[section_no]], ex=col_axis, ga=col_axis)
    result = [current]
    columns_here = jnp.arange(group_rows, dtype=jnp.int32)
    for section_no in range(levels - 1, -1, -1):
        picked = gathered.reshape((n_col * rows_dev,) + current.shape[1:])[row_ids[section_no]]
        spread = jnp.einsum(
            "tab,tan->tbn", factor_tiles[section_no], picked, preferred_element_type=jnp.float32
        )
        select = (col_ids[section_no][:, None] == columns_here[None, :]).astype(jnp.float32)
        column_sums = jnp.einsum("tj,tbn->jbn", select, spread, precision=HIGHEST)
        column_sums = column_sums.astype(jnp.bfloat16).reshape((n_row, rows_dev) + column_sums.shape[1:])
        if section_no > 0:
            current, gathered = level(4, column_sums, solved[section_no], [g_bwd[section_no]],
                                      ex=row_axis, ga=col_axis)
        else:
            current, _ = level(5, column_sums, solved[section_no], [g_bwd[section_no]], ex=row_axis)
        result.insert(0, current)
    return jnp.stack(result)


def solution(mesh):
    n_row, n_col = mesh.shape["row"], mesh.shape["col"]
    return jax.shard_map(
        functools.partial(solve_all, n_row, n_col),
        mesh=mesh,
        in_specs=(
            P(None, "row", None, "col"),
            P(None, "row", "col"),
            P(None, "row", "col"),
            P(None, ("col", "row"), None, None),
            P(None, None, ("col", "row")),
        ),
        out_specs=P(None, ("col", "row"), None, None),
        check_vma=False,
    )
```

```python
import functools

import jax
import jax.numpy as jnp
from jax import lax
from jax.experimental import pallas as pl
from jax.experimental.pallas import tpu as pltpu
from jax.sharding import PartitionSpec as P

MESH = pl.DeviceIdType.MESH
AXES = ("row", "col")
HIGHEST = lax.Precision.HIGHEST


def peer_id(axis, peer):
    return tuple(peer if name == axis else lax.axis_index(name) for name in AXES)


def level_kernel(ex, ga, applies, *refs):
    refs = list(refs)
    x_ref = refs.pop(0) if ex else None
    base_ref = refs.pop(0)
    g_refs = [refs.pop(0) for _ in applies]
    out_ref = refs.pop(0)
    gathered_ref = refs.pop(0) if ga else None
    if ex:
        held_x, ex_send, ex_recv = refs.pop(0), refs.pop(0), refs.pop(0)
    if ga:
        held_g, stage, ga_send, ga_recv = refs.pop(0), refs.pop(0), refs.pop(0), refs.pop(0)
    blocks = base_ref.shape[0]

    groups = [g for g in (ex, ga) if g]
    barrier = pltpu.get_barrier_semaphore()
    for axis, n in groups:
        me = lax.axis_index(axis)
        for k in range(1, n):
            pl.semaphore_signal(
                barrier, inc=1, device_id=peer_id(axis, lax.rem(me + k, n)), device_id_type=MESH
            )
    pl.semaphore_wait(barrier, sum(n - 1 for _, n in groups))

    def exchange_copies(kb):
        axis, n = ex
        me = lax.axis_index(axis)
        copies = []
        for k in range(1, n):
            peer = lax.rem(me + k, n)
            copy = pltpu.make_async_remote_copy(
                src_ref=x_ref.at[peer, kb],
                dst_ref=held_x.at[k, kb],
                send_sem=ex_send.at[kb, k],
                recv_sem=ex_recv.at[kb, k],
                device_id=peer_id(axis, peer),
                device_id_type=MESH,
            )
            copy.start()
            copies.append(copy)
        return copies

    gather_copies = []
    pending = exchange_copies(0) if ex else None
    for kb in range(blocks):
        value = base_ref[kb]
        if ex:
            axis, n = ex
            me = lax.axis_index(axis)
            copies = pending
            if kb + 1 < blocks:
                for copy in copies:
                    copy.wait_send()
                pending = exchange_copies(kb + 1)
            total = x_ref[me, kb].astype(jnp.float32)
            for k in range(1, n):
                copies[k - 1].wait_recv()
                total = total + held_x[k, kb].astype(jnp.float32)
            if kb + 1 == blocks:
                for copy in copies:
                    copy.wait_send()
            value = value - total
        for g_ref in g_refs:
            value = jnp.dot(g_ref[kb], value, precision=HIGHEST, preferred_element_type=jnp.float32)
        out_ref[kb] = value
        if ga:
            axis, n = ga
            me = lax.axis_index(axis)
            stage[kb] = value.astype(stage.dtype)
            for k in range(1, n):
                peer = lax.rem(me + k, n)
                copy = pltpu.make_async_remote_copy(
                    src_ref=stage.at[kb],
                    dst_ref=held_g.at[k, kb],
                    send_sem=ga_send.at[kb, k],
                    recv_sem=ga_recv.at[kb, k],
                    device_id=peer_id(axis, peer),
                    device_id_type=MESH,
                )
                copy.start()
                gather_copies.append((kb, k, copy))
            gathered_ref[me, kb] = value.astype(gathered_ref.dtype)
    if ga:
        axis, n = ga
        me = lax.axis_index(axis)
        for kb, k, copy in gather_copies:
            copy.wait()
            gathered_ref[lax.rem(me + n - k, n), kb] = held_g[k, kb]


def level(cid, x, base, gs, ex=None, ga=None):
    piece = base.shape
    vmem = pl.BlockSpec(memory_space=pltpu.VMEM)
    args = ([x] if ex else []) + [base] + list(gs)
    out_shape = [jax.ShapeDtypeStruct(piece, jnp.float32)]
    scratch = []
    if ex:
        scratch += [
            pltpu.VMEM((ex[1],) + piece, jnp.bfloat16),
            pltpu.SemaphoreType.DMA((piece[0], ex[1])),
            pltpu.SemaphoreType.DMA((piece[0], ex[1])),
        ]
    if ga:
        out_shape.append(jax.ShapeDtypeStruct((ga[1],) + piece, jnp.bfloat16))
        scratch += [
            pltpu.VMEM((ga[1],) + piece, jnp.bfloat16),
            pltpu.VMEM(piece, jnp.bfloat16),
            pltpu.SemaphoreType.DMA((piece[0], ga[1])),
            pltpu.SemaphoreType.DMA((piece[0], ga[1])),
        ]
    outs = pl.pallas_call(
        functools.partial(level_kernel, ex, ga, tuple(range(len(gs)))),
        out_shape=out_shape,
        in_specs=[vmem] * len(args),
        out_specs=[vmem] * len(out_shape),
        scratch_shapes=scratch,
        compiler_params=pltpu.CompilerParams(collective_id=cid, has_side_effects=True),
    )(*args)
    return outs if ga else (outs[0], None)


def solve_all(n_row, n_col, factor_tiles, tile_row, tile_col, right_sides, diag_inverse):
    levels = factor_tiles.shape[0]
    rows_dev = right_sides.shape[1]
    block = right_sides.shape[2]
    group_rows = rows_dev * n_row
    row_ids = tile_row[:, :, 0]
    col_ids = tile_col[:, :, 0]
    split = diag_inverse.reshape(levels + 1, block, rows_dev, block)
    g_fwd = split.transpose(0, 2, 3, 1)
    g_bwd = split.transpose(0, 2, 1, 3)
    row_axis, col_axis = ("row", n_row), ("col", n_col)

    current, gathered = level(1, None, right_sides[0], [g_fwd[0]], ga=row_axis)
    solved = [current]
    for section_no in range(1, levels + 1):
        picked = gathered.reshape((group_rows,) + current.shape[1:])[col_ids[section_no - 1]]
        products = jnp.einsum(
            "tab,tbn->tan", factor_tiles[section_no - 1], picked, preferred_element_type=jnp.float32
        )
        targets = row_ids[section_no - 1]
        places = jnp.arange(n_col * rows_dev, dtype=jnp.int32)
        select = (targets[:, None] == places[None, :]).astype(jnp.float32)
        terms = jnp.einsum("tq,tan->qan", select, products, precision=HIGHEST)
        terms = terms.astype(jnp.bfloat16).reshape((n_col, rows_dev) + terms.shape[1:])
        if section_no < levels:
            current, gathered = level(2, terms, right_sides[section_no], [g_fwd[section_no]],
                                      ex=col_axis, ga=row_axis)
            solved.append(current)
        else:
            current, gathered = level(3, terms, right_sides[section_no],
                                      [g_fwd[section_no], g_bwd[section_no]], ex=col_axis, ga=col_axis)
    result = [current]
    columns_here = jnp.arange(group_rows, dtype=jnp.int32)
    for section_no in range(levels - 1, -1, -1):
        picked = gathered.reshape((n_col * rows_dev,) + current.shape[1:])[row_ids[section_no]]
        spread = jnp.einsum(
            "tab,tan->tbn", factor_tiles[section_no], picked, preferred_element_type=jnp.float32
        )
        select = (col_ids[section_no][:, None] == columns_here[None, :]).astype(jnp.float32)
        column_sums = jnp.einsum("tj,tbn->jbn", select, spread, precision=HIGHEST)
        column_sums = column_sums.astype(jnp.bfloat16).reshape((n_row, rows_dev) + column_sums.shape[1:])
        if section_no > 0:
            current, gathered = level(4, column_sums, solved[section_no], [g_bwd[section_no]],
                                      ex=row_axis, ga=col_axis)
        else:
            current, _ = level(5, column_sums, solved[section_no], [g_bwd[section_no]], ex=row_axis)
        result.insert(0, current)
    return jnp.stack(result)


def solution(mesh):
    n_row, n_col = mesh.shape["row"], mesh.shape["col"]
    return jax.shard_map(
        functools.partial(solve_all, n_row, n_col),
        mesh=mesh,
        in_specs=(
            P(None, "row", None, "col"),
            P(None, "row", "col"),
            P(None, "row", "col"),
            P(None, ("col", "row"), None, None),
            P(None, None, ("col", "row")),
        ),
        out_specs=P(None, ("col", "row"), None, None),
        check_vma=False,
    )
```

```python
import functools

import jax
import jax.numpy as jnp
from jax import lax
from jax.experimental import pallas as pl
from jax.experimental.pallas import tpu as pltpu
from jax.sharding import PartitionSpec as P

MESH = pl.DeviceIdType.MESH
AXES = ("row", "col")
HIGHEST = lax.Precision.HIGHEST


def peer_id(axis, peer):
    return tuple(peer if name == axis else lax.axis_index(name) for name in AXES)


def level_kernel(ex, ga, applies, *refs):
    refs = list(refs)
    x_ref = refs.pop(0) if ex else None
    base_ref = refs.pop(0)
    g_refs = [refs.pop(0) for _ in applies]
    if ga:
        ids_ref, tiles_ref = refs.pop(0), refs.pop(0)
    out_ref = refs.pop(0)
    products_ref = refs.pop(0) if ga else None
    if ex:
        held_x, ex_send, ex_recv = refs.pop(0), refs.pop(0), refs.pop(0)
    if ga:
        held_g, stage, ga_send, ga_recv = refs.pop(0), refs.pop(0), refs.pop(0), refs.pop(0)
    blocks = base_ref.shape[0]

    groups = [g for g in (ex, ga) if g]
    barrier = pltpu.get_barrier_semaphore()
    for axis, n in groups:
        me = lax.axis_index(axis)
        for k in range(1, n):
            pl.semaphore_signal(
                barrier, inc=1, device_id=peer_id(axis, lax.rem(me + k, n)), device_id_type=MESH
            )
    pl.semaphore_wait(barrier, sum(n - 1 for _, n in groups))

    def exchange_copies(kb):
        axis, n = ex
        me = lax.axis_index(axis)
        copies = []
        for k in range(1, n):
            peer = lax.rem(me + k, n)
            copy = pltpu.make_async_remote_copy(
                src_ref=x_ref.at[peer, kb],
                dst_ref=held_x.at[k, kb],
                send_sem=ex_send.at[kb, k],
                recv_sem=ex_recv.at[kb, k],
                device_id=peer_id(axis, peer),
                device_id_type=MESH,
            )
            copy.start()
            copies.append(copy)
        return copies

    gather_copies = []
    pending = exchange_copies(0) if ex else None
    for kb in range(blocks):
        value = base_ref[kb]
        if ex:
            axis, n = ex
            me = lax.axis_index(axis)
            copies = pending
            if kb + 1 < blocks:
                for copy in copies:
                    copy.wait_send()
                pending = exchange_copies(kb + 1)
            total = x_ref[me, kb].astype(jnp.float32)
            for k in range(1, n):
                copies[k - 1].wait_recv()
                total = total + held_x[k, kb].astype(jnp.float32)
            if kb + 1 == blocks:
                for copy in copies:
                    copy.wait_send()
            value = value - total
        for g_ref in g_refs:
            value = jnp.dot(g_ref[kb], value, precision=HIGHEST, preferred_element_type=jnp.float32)
        out_ref[kb] = value
        if ga:
            axis, n = ga
            me = lax.axis_index(axis)
            stage[kb] = value.astype(stage.dtype)
            for k in range(1, n):
                peer = lax.rem(me + k, n)
                copy = pltpu.make_async_remote_copy(
                    src_ref=stage.at[kb],
                    dst_ref=held_g.at[me * blocks + kb],
                    send_sem=ga_send.at[kb, k],
                    recv_sem=ga_recv.at[kb, k],
                    device_id=peer_id(axis, peer),
                    device_id_type=MESH,
                )
                copy.start()
                gather_copies.append(copy)
            held_g[me * blocks + kb] = value.astype(held_g.dtype)
    if ga:
        for copy in gather_copies:
            copy.wait()
        for t in range(tiles_ref.shape[0]):
            products_ref[t] = jnp.dot(
                tiles_ref[t], held_g[ids_ref[t]], preferred_element_type=jnp.float32
            )


def level(cid, x, base, gs, ex=None, ga=None, ids=None, tiles=None):
    piece = base.shape
    vmem = pl.BlockSpec(memory_space=pltpu.VMEM)
    smem = pl.BlockSpec(memory_space=pltpu.SMEM)
    args = ([x] if ex else []) + [base] + list(gs)
    specs = [vmem] * len(args)
    out_shape = [jax.ShapeDtypeStruct(piece, jnp.float32)]
    scratch = []
    if ex:
        scratch += [
            pltpu.VMEM((ex[1],) + piece, jnp.bfloat16),
            pltpu.SemaphoreType.DMA((piece[0], ex[1])),
            pltpu.SemaphoreType.DMA((piece[0], ex[1])),
        ]
    if ga:
        args += [ids, tiles]
        specs += [smem, vmem]
        out_shape.append(jax.ShapeDtypeStruct(tiles.shape[:2] + piece[2:], jnp.float32))
        scratch += [
            pltpu.VMEM((ga[1] * piece[0],) + piece[1:], jnp.bfloat16),
            pltpu.VMEM(piece, jnp.bfloat16),
            pltpu.SemaphoreType.DMA((piece[0], ga[1])),
            pltpu.SemaphoreType.DMA((piece[0], ga[1])),
        ]
    outs = pl.pallas_call(
        functools.partial(level_kernel, ex, ga, tuple(range(len(gs)))),
        out_shape=out_shape,
        in_specs=specs,
        out_specs=[vmem] * len(out_shape),
        scratch_shapes=scratch,
        compiler_params=pltpu.CompilerParams(collective_id=cid, has_side_effects=True),
    )(*args)
    return outs if ga else (outs[0], None)


def solve_all(n_row, n_col, factor_tiles, tile_row, tile_col, right_sides, diag_inverse):
    levels = factor_tiles.shape[0]
    rows_dev = right_sides.shape[1]
    block = right_sides.shape[2]
    group_rows = rows_dev * n_row
    row_ids = tile_row[:, :, 0]
    col_ids = tile_col[:, :, 0]
    split = diag_inverse.reshape(levels + 1, block, rows_dev, block)
    g_fwd = split.transpose(0, 2, 3, 1)
    g_bwd = split.transpose(0, 2, 1, 3)
    row_axis, col_axis = ("row", n_row), ("col", n_col)
    tiles_t = jnp.swapaxes(factor_tiles, 2, 3)
    places = jnp.arange(n_col * rows_dev, dtype=jnp.int32)
    columns_here = jnp.arange(group_rows, dtype=jnp.int32)

    def forward_terms(products, section_no):
        select = (row_ids[section_no][:, None] == places[None, :]).astype(jnp.float32)
        terms = jnp.einsum("tq,tan->qan", select, products, precision=HIGHEST)
        return terms.astype(jnp.bfloat16).reshape((n_col, rows_dev) + terms.shape[1:])

    def backward_terms(products, section_no):
        select = (col_ids[section_no][:, None] == columns_here[None, :]).astype(jnp.float32)
        sums = jnp.einsum("tj,tbn->jbn", select, products, precision=HIGHEST)
        return sums.astype(jnp.bfloat16).reshape((n_row, rows_dev) + sums.shape[1:])

    current, products = level(1, None, right_sides[0], [g_fwd[0]], ga=row_axis,
                              ids=col_ids[0], tiles=factor_tiles[0])
    solved = [current]
    for section_no in range(1, levels + 1):
        terms = forward_terms(products, section_no - 1)
        if section_no < levels:
            current, products = level(2, terms, right_sides[section_no], [g_fwd[section_no]],
                                      ex=col_axis, ga=row_axis,
                                      ids=col_ids[section_no], tiles=factor_tiles[section_no])
            solved.append(current)
        else:
            current, products = level(3, terms, right_sides[section_no],
                                      [g_fwd[section_no], g_bwd[section_no]], ex=col_axis, ga=col_axis,
                                      ids=row_ids[levels - 1], tiles=tiles_t[levels - 1])
    result = [current]
    for section_no in range(levels - 1, -1, -1):
        column_sums = backward_terms(products, section_no)
        if section_no > 0:
            current, products = level(4, column_sums, solved[section_no], [g_bwd[section_no]],
                                      ex=row_axis, ga=col_axis,
                                      ids=row_ids[section_no - 1], tiles=tiles_t[section_no - 1])
        else:
            current, _ = level(5, column_sums, solved[section_no], [g_bwd[section_no]], ex=row_axis)
        result.insert(0, current)
    return jnp.stack(result)


def solution(mesh):
    n_row, n_col = mesh.shape["row"], mesh.shape["col"]
    return jax.shard_map(
        functools.partial(solve_all, n_row, n_col),
        mesh=mesh,
        in_specs=(
            P(None, "row", None, "col"),
            P(None, "row", "col"),
            P(None, "row", "col"),
            P(None, ("col", "row"), None, None),
            P(None, None, ("col", "row")),
        ),
        out_specs=P(None, ("col", "row"), None, None),
        check_vma=False,
    )
```

```python
import functools

import jax
import jax.numpy as jnp
from jax import lax
from jax.experimental import pallas as pl
from jax.experimental.pallas import tpu as pltpu
from jax.sharding import PartitionSpec as P

MESH = pl.DeviceIdType.MESH
AXES = ("row", "col")
HIGHEST = lax.Precision.HIGHEST


def peer_id(axis, peer):
    return tuple(peer if name == axis else lax.axis_index(name) for name in AXES)


def level_kernel(ex, ga, applies, *refs):
    refs = list(refs)
    x_ref = refs.pop(0) if ex else None
    base_ref = refs.pop(0)
    g_refs = [refs.pop(0) for _ in applies]
    if ga:
        ids_ref, tiles_ref, key_ref, first_ref, has_ref = [refs.pop(0) for _ in range(5)]
    out_ref = refs.pop(0)
    terms_ref = refs.pop(0) if ga else None
    if ex:
        held_x, ex_send, ex_recv = refs.pop(0), refs.pop(0), refs.pop(0)
    if ga:
        held_g, stage, ga_send, ga_recv, prod, group = [refs.pop(0) for _ in range(6)]
    blocks = base_ref.shape[0]

    groups = [g for g in (ex, ga) if g]
    barrier = pltpu.get_barrier_semaphore()
    for axis, n in groups:
        me = lax.axis_index(axis)
        for k in range(1, n):
            pl.semaphore_signal(
                barrier, inc=1, device_id=peer_id(axis, lax.rem(me + k, n)), device_id_type=MESH
            )
    pl.semaphore_wait(barrier, sum(n - 1 for _, n in groups))

    def exchange_copies(kb):
        axis, n = ex
        me = lax.axis_index(axis)
        copies = []
        for k in range(1, n):
            peer = lax.rem(me + k, n)
            copy = pltpu.make_async_remote_copy(
                src_ref=x_ref.at[peer, kb],
                dst_ref=held_x.at[k, kb],
                send_sem=ex_send.at[kb, k],
                recv_sem=ex_recv.at[kb, k],
                device_id=peer_id(axis, peer),
                device_id_type=MESH,
            )
            copy.start()
            copies.append(copy)
        return copies

    gather_copies = []
    pending = exchange_copies(0) if ex else None
    for kb in range(blocks):
        value = base_ref[kb]
        if ex:
            axis, n = ex
            me = lax.axis_index(axis)
            copies = pending
            if kb + 1 < blocks:
                for copy in copies:
                    copy.wait_send()
                pending = exchange_copies(kb + 1)
            total = x_ref[me, kb].astype(jnp.float32)
            for k in range(1, n):
                copies[k - 1].wait_recv()
                total = total + held_x[k, kb].astype(jnp.float32)
            if kb + 1 == blocks:
                for copy in copies:
                    copy.wait_send()
            value = value - total
        for g_ref in g_refs:
            value = jnp.dot(g_ref[kb], value, precision=HIGHEST, preferred_element_type=jnp.float32)
        out_ref[kb] = value
        if ga:
            axis, n = ga
            me = lax.axis_index(axis)
            stage[kb] = value.astype(stage.dtype)
            for k in range(1, n):
                peer = lax.rem(me + k, n)
                copy = pltpu.make_async_remote_copy(
                    src_ref=stage.at[kb],
                    dst_ref=held_g.at[me * blocks + kb],
                    send_sem=ga_send.at[kb, k],
                    recv_sem=ga_recv.at[kb, k],
                    device_id=peer_id(axis, peer),
                    device_id_type=MESH,
                )
                copy.start()
                gather_copies.append(copy)
            held_g[me * blocks + kb] = value.astype(held_g.dtype)
    if ga:
        for copy in gather_copies:
            copy.wait()
        tiles = tiles_ref.shape[0]

        def product(t, carry):
            prod[t] = jnp.dot(tiles_ref[t], held_g[ids_ref[t]], preferred_element_type=jnp.float32)
            return carry

        lax.fori_loop(0, tiles, product, 0)

        def grouping(t, carry):
            key = key_ref[t]
            acc = jnp.zeros(prod.shape[1:], jnp.float32)
            for other in range(tiles):
                acc = acc + jnp.where(key_ref[other] == key, prod[other], 0.0)
            group[t] = acc
            return carry

        lax.fori_loop(0, tiles, grouping, 0)

        def place(q, carry):
            terms_ref[q] = (group[first_ref[q]] * has_ref[q]).astype(terms_ref.dtype)
            return carry

        lax.fori_loop(0, terms_ref.shape[0], place, 0)


def level(cid, x, base, gs, ex=None, ga=None, ids=None, tiles=None, keys=None):
    piece = base.shape
    vmem = pl.BlockSpec(memory_space=pltpu.VMEM)
    smem = pl.BlockSpec(memory_space=pltpu.SMEM)
    args = ([x] if ex else []) + [base] + list(gs)
    specs = [vmem] * len(args)
    out_shape = [jax.ShapeDtypeStruct(piece, jnp.float32)]
    scratch = []
    if ex:
        scratch += [
            pltpu.VMEM((ex[1],) + piece, jnp.bfloat16),
            pltpu.SemaphoreType.DMA((piece[0], ex[1])),
            pltpu.SemaphoreType.DMA((piece[0], ex[1])),
        ]
    if ga:
        key, first, has = keys
        args += [ids, tiles, key, first, has]
        specs += [smem, vmem, smem, smem, smem]
        out_shape.append(jax.ShapeDtypeStruct(first.shape + piece[1:], jnp.bfloat16))
        scratch += [
            pltpu.VMEM((ga[1] * piece[0],) + piece[1:], jnp.bfloat16),
            pltpu.VMEM(piece, jnp.bfloat16),
            pltpu.SemaphoreType.DMA((piece[0], ga[1])),
            pltpu.SemaphoreType.DMA((piece[0], ga[1])),
            pltpu.VMEM(tiles.shape[:2] + piece[2:], jnp.float32),
            pltpu.VMEM(tiles.shape[:2] + piece[2:], jnp.float32),
        ]
    outs = pl.pallas_call(
        functools.partial(level_kernel, ex, ga, tuple(range(len(gs)))),
        out_shape=out_shape,
        in_specs=specs,
        out_specs=[vmem] * len(out_shape),
        scratch_shapes=scratch,
        compiler_params=pltpu.CompilerParams(collective_id=cid, has_side_effects=True),
    )(*args)
    return outs if ga else (outs[0], None)


def solve_all(n_row, n_col, factor_tiles, tile_row, tile_col, right_sides, diag_inverse):
    levels = factor_tiles.shape[0]
    rows_dev = right_sides.shape[1]
    block = right_sides.shape[2]
    group_rows = rows_dev * n_row
    row_ids = tile_row[:, :, 0]
    col_ids = tile_col[:, :, 0]
    split = diag_inverse.reshape(levels + 1, block, rows_dev, block)
    g_fwd = split.transpose(0, 2, 3, 1)
    g_bwd = split.transpose(0, 2, 1, 3)
    row_axis, col_axis = ("row", n_row), ("col", n_col)
    tiles_t = jnp.swapaxes(factor_tiles, 2, 3)

    def grouping(keys, size):
        hits = keys[:, :, None] == jnp.arange(size, dtype=jnp.int32)[None, None, :]
        return keys, jnp.argmax(hits, axis=1).astype(jnp.int32), jnp.any(hits, axis=1).astype(jnp.float32)

    fwd_keys = grouping(row_ids, n_col * rows_dev)
    bwd_keys = grouping(col_ids, group_rows)

    def keys_of(which, section_no):
        return tuple(k[section_no] for k in which)

    def as_pieces(terms, n):
        return terms.reshape((n, rows_dev) + terms.shape[1:])

    current, terms = level(1, None, right_sides[0], [g_fwd[0]], ga=row_axis,
                           ids=col_ids[0], tiles=factor_tiles[0], keys=keys_of(fwd_keys, 0))
    solved = [current]
    for section_no in range(1, levels + 1):
        terms = as_pieces(terms, n_col)
        if section_no < levels:
            current, terms = level(2, terms, right_sides[section_no], [g_fwd[section_no]],
                                   ex=col_axis, ga=row_axis, ids=col_ids[section_no],
                                   tiles=factor_tiles[section_no], keys=keys_of(fwd_keys, section_no))
            solved.append(current)
        else:
            current, terms = level(3, terms, right_sides[section_no],
                                   [g_fwd[section_no], g_bwd[section_no]], ex=col_axis, ga=col_axis,
                                   ids=row_ids[levels - 1], tiles=tiles_t[levels - 1],
                                   keys=keys_of(bwd_keys, levels - 1))
    result = [current]
    for section_no in range(levels - 1, -1, -1):
        terms = as_pieces(terms, n_row)
        if section_no > 0:
            current, terms = level(4, terms, solved[section_no], [g_bwd[section_no]],
                                   ex=row_axis, ga=col_axis, ids=row_ids[section_no - 1],
                                   tiles=tiles_t[section_no - 1], keys=keys_of(bwd_keys, section_no - 1))
        else:
            current, _ = level(5, terms, solved[section_no], [g_bwd[section_no]], ex=row_axis)
        result.insert(0, current)
    return jnp.stack(result)


def solution(mesh):
    n_row, n_col = mesh.shape["row"], mesh.shape["col"]
    return jax.shard_map(
        functools.partial(solve_all, n_row, n_col),
        mesh=mesh,
        in_specs=(
            P(None, "row", None, "col"),
            P(None, "row", "col"),
            P(None, "row", "col"),
            P(None, ("col", "row"), None, None),
            P(None, None, ("col", "row")),
        ),
        out_specs=P(None, ("col", "row"), None, None),
        check_vma=False,
    )
```

```python
import functools

import jax
import jax.numpy as jnp
from jax import lax
from jax.experimental import pallas as pl
from jax.experimental.pallas import tpu as pltpu
from jax.sharding import PartitionSpec as P

MESH = pl.DeviceIdType.MESH
AXES = ("row", "col")
HIGHEST = lax.Precision.HIGHEST


def peer_id(axis, peer):
    return tuple(peer if name == axis else lax.axis_index(name) for name in AXES)


def phase(cfg, base, gs, out, x, ids, tiles, keys, bufs):
    ex, ga = cfg
    blocks = base.shape[0]

    def exchange_copies(kb):
        axis, n = ex
        held_x, ex_send, ex_recv = bufs["ex"]
        me = lax.axis_index(axis)
        copies = []
        for k in range(1, n):
            peer = lax.rem(me + k, n)
            copy = pltpu.make_async_remote_copy(
                src_ref=x.at[peer, kb],
                dst_ref=held_x.at[k, kb],
                send_sem=ex_send.at[kb, k],
                recv_sem=ex_recv.at[kb, k],
                device_id=peer_id(axis, peer),
                device_id_type=MESH,
            )
            copy.start()
            copies.append(copy)
        return copies

    gather_copies = []
    pending = exchange_copies(0) if ex else None
    for kb in range(blocks):
        value = base[kb]
        if ex:
            axis, n = ex
            held_x = bufs["ex"][0]
            me = lax.axis_index(axis)
            copies = pending
            if kb + 1 < blocks:
                for copy in copies:
                    copy.wait_send()
                pending = exchange_copies(kb + 1)
            total = x[me, kb].astype(jnp.float32)
            for k in range(1, n):
                copies[k - 1].wait_recv()
                total = total + held_x[k, kb].astype(jnp.float32)
            if kb + 1 == blocks:
                for copy in copies:
                    copy.wait_send()
            value = value - total
        for g in gs:
            value = jnp.dot(g[kb], value, precision=HIGHEST, preferred_element_type=jnp.float32)
        out[kb] = value
        if ga:
            axis, n = ga
            held_g, stage, ga_send, ga_recv, _ = bufs["ga"]
            me = lax.axis_index(axis)
            stage[kb] = value.astype(stage.dtype)
            for k in range(1, n):
                peer = lax.rem(me + k, n)
                copy = pltpu.make_async_remote_copy(
                    src_ref=stage.at[kb],
                    dst_ref=held_g.at[me * blocks + kb],
                    send_sem=ga_send.at[kb, k],
                    recv_sem=ga_recv.at[kb, k],
                    device_id=peer_id(axis, peer),
                    device_id_type=MESH,
                )
                copy.start()
                gather_copies.append(copy)
            held_g[me * blocks + kb] = value.astype(held_g.dtype)
    if not ga:
        return
    held_g, _, _, _, terms = bufs["ga"]
    prod, group = bufs["work"]
    for copy in gather_copies:
        copy.wait()
    n_tiles = prod.shape[0]

    def product(t, carry):
        prod[t] = jnp.dot(tiles[t], held_g[ids[t]], preferred_element_type=jnp.float32)
        return carry

    lax.fori_loop(0, n_tiles, product, 0)
    key, first, has = keys

    def grouping(t, carry):
        mine = key[t]
        acc = jnp.zeros(prod.shape[1:], jnp.float32)
        for other in range(n_tiles):
            acc = acc + jnp.where(key[other] == mine, prod[other], 0.0)
        group[t] = acc
        return carry

    lax.fori_loop(0, n_tiles, grouping, 0)

    def place(q, carry):
        terms[q // blocks, q % blocks] = (group[first[q]] * has[q]).astype(terms.dtype)
        return carry

    lax.fori_loop(0, terms.shape[0] * blocks, place, 0)


def solve_kernel(plan, *refs):
    refs = list(refs)
    (rhs, g_fwd, g_bwd, tiles, tiles_t, row_ids, col_ids,
     fwd_first, fwd_has, bwd_first, bwd_has, out, prod, group) = [refs.pop(0) for _ in range(14)]
    bufs = []
    for ex, ga in plan:
        entry = {"work": (prod, group)}
        if ex:
            entry["ex"] = tuple(refs.pop(0) for _ in range(3))
        if ga:
            entry["ga"] = tuple(refs.pop(0) for _ in range(5))
        bufs.append(entry)

    peers = {}
    for ex, ga in plan:
        for group_axis in (ex, ga):
            if group_axis:
                peers[group_axis[0]] = group_axis[1]
    barrier = pltpu.get_barrier_semaphore()
    for axis, n in peers.items():
        me = lax.axis_index(axis)
        for k in range(1, n):
            pl.semaphore_signal(
                barrier, inc=1, device_id=peer_id(axis, lax.rem(me + k, n)), device_id_type=MESH
            )
    pl.semaphore_wait(barrier, sum(n - 1 for n in peers.values()))

    levels = tiles.shape[0]

    def fwd_keys(s):
        return row_ids.at[s], fwd_first.at[s], fwd_has.at[s]

    def bwd_keys(s):
        return col_ids.at[s], bwd_first.at[s], bwd_has.at[s]

    previous = None
    for p, cfg in enumerate(plan):
        x = previous
        if p < levels:
            phase(cfg, rhs.at[p], [g_fwd.at[p]], out.at[p], x, col_ids.at[p], tiles.at[p],
                  fwd_keys(p), bufs[p])
        elif p == levels:
            phase(cfg, rhs.at[p], [g_fwd.at[p], g_bwd.at[p]], out.at[p], x, row_ids.at[p - 1],
                  tiles_t.at[p - 1], bwd_keys(p - 1), bufs[p])
        else:
            s = 2 * levels - p
            if s > 0:
                phase(cfg, out.at[s], [g_bwd.at[s]], out.at[s], x, row_ids.at[s - 1], tiles_t.at[s - 1],
                      bwd_keys(s - 1), bufs[p])
            else:
                phase(cfg, out.at[s], [g_bwd.at[s]], out.at[s], x, None, None, None, bufs[p])
        if cfg[1]:
            previous = bufs[p]["ga"][4]


def solve_all(n_row, n_col, factor_tiles, tile_row, tile_col, right_sides, diag_inverse):
    levels = factor_tiles.shape[0]
    rows_dev = right_sides.shape[1]
    block = right_sides.shape[2]
    group_rows = rows_dev * n_row
    row_ids = tile_row[:, :, 0]
    col_ids = tile_col[:, :, 0]
    split = diag_inverse.reshape(levels + 1, block, rows_dev, block)
    g_fwd = split.transpose(0, 2, 3, 1)
    g_bwd = split.transpose(0, 2, 1, 3)
    tiles_t = jnp.swapaxes(factor_tiles, 2, 3)
    row_axis, col_axis = ("row", n_row), ("col", n_col)

    def grouping(keys, size):
        hits = keys[:, :, None] == jnp.arange(size, dtype=jnp.int32)[None, None, :]
        return jnp.argmax(hits, axis=1).astype(jnp.int32), jnp.any(hits, axis=1).astype(jnp.float32)

    fwd_first, fwd_has = grouping(row_ids, n_col * rows_dev)
    bwd_first, bwd_has = grouping(col_ids, group_rows)

    plan = [(None, row_axis)]
    plan += [(col_axis, row_axis)] * (levels - 1)
    plan += [(col_axis, col_axis)]
    plan += [(row_axis, col_axis)] * (levels - 1)
    plan += [(row_axis, None)]

    piece = right_sides.shape[1:]
    n_tiles = factor_tiles.shape[1]
    vmem = pl.BlockSpec(memory_space=pltpu.VMEM)
    smem = pl.BlockSpec(memory_space=pltpu.SMEM)
    scratch = [
        pltpu.VMEM((n_tiles,) + piece[1:], jnp.float32),
        pltpu.VMEM((n_tiles,) + piece[1:], jnp.float32),
    ]
    for ex, ga in plan:
        if ex:
            scratch += [
                pltpu.VMEM((ex[1],) + piece, jnp.bfloat16),
                pltpu.SemaphoreType.DMA((rows_dev, ex[1])),
                pltpu.SemaphoreType.DMA((rows_dev, ex[1])),
            ]
        if ga:
            targets = n_col if ga[0] == "row" else n_row
            scratch += [
                pltpu.VMEM((ga[1] * rows_dev,) + piece[1:], jnp.bfloat16),
                pltpu.VMEM(piece, jnp.bfloat16),
                pltpu.SemaphoreType.DMA((rows_dev, ga[1])),
                pltpu.SemaphoreType.DMA((rows_dev, ga[1])),
                pltpu.VMEM((targets,) + piece, jnp.bfloat16),
            ]
    args = [right_sides, g_fwd, g_bwd, factor_tiles, tiles_t, row_ids, col_ids,
            fwd_first, fwd_has, bwd_first, bwd_has]
    specs = [vmem] * 5 + [smem] * 6
    return pl.pallas_call(
        functools.partial(solve_kernel, plan),
        out_shape=jax.ShapeDtypeStruct(right_sides.shape, jnp.float32),
        in_specs=specs,
        out_specs=vmem,
        scratch_shapes=scratch,
        compiler_params=pltpu.CompilerParams(collective_id=1, has_side_effects=True),
    )(*args)


def solution(mesh):
    n_row, n_col = mesh.shape["row"], mesh.shape["col"]
    return jax.shard_map(
        functools.partial(solve_all, n_row, n_col),
        mesh=mesh,
        in_specs=(
            P(None, "row", None, "col"),
            P(None, "row", "col"),
            P(None, "row", "col"),
            P(None, ("col", "row"), None, None),
            P(None, None, ("col", "row")),
        ),
        out_specs=P(None, ("col", "row"), None, None),
        check_vma=False,
    )
```

```python
import functools

import jax
import jax.numpy as jnp
from jax import lax
from jax.experimental import pallas as pl
from jax.experimental.pallas import tpu as pltpu
from jax.sharding import PartitionSpec as P

MESH = pl.DeviceIdType.MESH
AXES = ("row", "col")
HIGHEST = lax.Precision.HIGHEST


def peer_id(axis, peer):
    return tuple(peer if name == axis else lax.axis_index(name) for name in AXES)


def phase(cfg, base, gs, out, x, ids, tiles, keys, bufs, tiles_transposed=False, meanwhile=None):
    ex, ga = cfg
    blocks = base.shape[0]

    def exchange_copies(kb):
        axis, n = ex
        held_x, ex_send, ex_recv = bufs["ex"]
        me = lax.axis_index(axis)
        copies = []
        for k in range(1, n):
            peer = lax.rem(me + k, n)
            copy = pltpu.make_async_remote_copy(
                src_ref=x.at[peer, kb],
                dst_ref=held_x.at[k, kb],
                send_sem=ex_send.at[kb, k],
                recv_sem=ex_recv.at[kb, k],
                device_id=peer_id(axis, peer),
                device_id_type=MESH,
            )
            copy.start()
            copies.append(copy)
        return copies

    gather_copies = []
    pending = exchange_copies(0) if ex else None
    for kb in range(blocks):
        value = base[kb]
        if ex:
            axis, n = ex
            held_x = bufs["ex"][0]
            me = lax.axis_index(axis)
            copies = pending
            if kb + 1 < blocks:
                for copy in copies:
                    copy.wait_send()
                pending = exchange_copies(kb + 1)
            total = x[me, kb].astype(jnp.float32)
            for k in range(1, n):
                copies[k - 1].wait_recv()
                total = total + held_x[k, kb].astype(jnp.float32)
            if kb + 1 == blocks:
                for copy in copies:
                    copy.wait_send()
            value = value - total
        width = value.shape[0]
        for diag, transposed in gs:
            d = diag[:, pl.ds(kb * width, width)]
            contract = 0 if transposed else 1
            value = lax.dot_general(d, value, (((contract,), (0,)), ((), ())),
                                    precision=HIGHEST, preferred_element_type=jnp.float32)
        out[kb] = value
        if ga:
            axis, n = ga
            held_g, stage, ga_send, ga_recv, _ = bufs["ga"]
            me = lax.axis_index(axis)
            stage[kb] = value.astype(stage.dtype)
            for k in range(1, n):
                peer = lax.rem(me + k, n)
                copy = pltpu.make_async_remote_copy(
                    src_ref=stage.at[kb],
                    dst_ref=held_g.at[me * blocks + kb],
                    send_sem=ga_send.at[kb, k],
                    recv_sem=ga_recv.at[kb, k],
                    device_id=peer_id(axis, peer),
                    device_id_type=MESH,
                )
                copy.start()
                gather_copies.append(copy)
            held_g[me * blocks + kb] = value.astype(held_g.dtype)
    if not ga:
        return
    held_g, _, _, _, terms = bufs["ga"]
    prod, group = bufs["work"]
    if meanwhile is not None:
        meanwhile()
    for copy in gather_copies:
        copy.wait()
    n_tiles = prod.shape[0]

    def product(t, carry):
        contract = 0 if tiles_transposed else 1
        prod[t] = lax.dot_general(tiles[t], held_g[ids[t, 0]], (((contract,), (0,)), ((), ())),
                                  preferred_element_type=jnp.float32)
        return carry

    lax.fori_loop(0, n_tiles, product, 0)
    key, first, has = keys

    def grouping(t, carry):
        mine = key[t, 0]
        acc = jnp.zeros(prod.shape[1:], jnp.float32)
        for other in range(n_tiles):
            acc = acc + jnp.where(key[other, 0] == mine, prod[other], 0.0)
        group[t] = acc
        return carry

    lax.fori_loop(0, n_tiles, grouping, 0)

    def place(q, carry):
        terms[q // blocks, q % blocks] = jnp.where(has[q] != 0, group[first[q]], 0.0).astype(terms.dtype)
        return carry

    lax.fori_loop(0, terms.shape[0] * blocks, place, 0)


def fill_tables(key, first, has):
    n_tiles = key.shape[1]
    for s in range(key.shape[0]):

        def body(q, carry, s=s):
            found = jnp.int32(0)
            hit_any = jnp.int32(0)
            for t in reversed(range(n_tiles)):
                hit = key[s, t, 0] == q
                found = jnp.where(hit, jnp.int32(t), found)
                hit_any = jnp.where(hit, jnp.int32(1), hit_any)
            first[s, q] = found
            has[s, q] = hit_any
            return carry

        lax.fori_loop(0, first.shape[1], body, 0)


def solve_kernel(plan, *refs):
    refs = list(refs)
    (rhs, diag, tiles, row_ids, col_ids, out, prod, group,
     fwd_first, fwd_has, bwd_first, bwd_has) = [refs.pop(0) for _ in range(12)]
    bufs = []
    for ex, ga in plan:
        entry = {"work": (prod, group)}
        if ex:
            entry["ex"] = tuple(refs.pop(0) for _ in range(3))
        if ga:
            entry["ga"] = tuple(refs.pop(0) for _ in range(5))
        bufs.append(entry)

    peers = {}
    for ex, ga in plan:
        for group_axis in (ex, ga):
            if group_axis:
                peers[group_axis[0]] = group_axis[1]
    barrier = pltpu.get_barrier_semaphore()
    for axis, n in peers.items():
        me = lax.axis_index(axis)
        for k in range(1, n):
            pl.semaphore_signal(
                barrier, inc=1, device_id=peer_id(axis, lax.rem(me + k, n)), device_id_type=MESH
            )
    pl.semaphore_wait(barrier, sum(n - 1 for n in peers.values()))

    levels = tiles.shape[0]

    def tables():
        fill_tables(row_ids, fwd_first, fwd_has)
        fill_tables(col_ids, bwd_first, bwd_has)

    def fwd_keys(s):
        return row_ids.at[s], fwd_first.at[s], fwd_has.at[s]

    def bwd_keys(s):
        return col_ids.at[s], bwd_first.at[s], bwd_has.at[s]

    previous = None
    for p, cfg in enumerate(plan):
        x = previous
        if p < levels:
            phase(cfg, rhs.at[p], [(diag.at[p], True)], out.at[p], x, col_ids.at[p], tiles.at[p],
                  fwd_keys(p), bufs[p], meanwhile=tables if p == 0 else None)
        elif p == levels:
            phase(cfg, rhs.at[p], [(diag.at[p], True), (diag.at[p], False)], out.at[p], x,
                  row_ids.at[p - 1], tiles.at[p - 1], bwd_keys(p - 1), bufs[p], tiles_transposed=True)
        else:
            s = 2 * levels - p
            if s > 0:
                phase(cfg, out.at[s], [(diag.at[s], False)], out.at[s], x, row_ids.at[s - 1],
                      tiles.at[s - 1], bwd_keys(s - 1), bufs[p], tiles_transposed=True)
            else:
                phase(cfg, out.at[s], [(diag.at[s], False)], out.at[s], x, None, None, None, bufs[p])
        if cfg[1]:
            previous = bufs[p]["ga"][4]


def solve_all(n_row, n_col, factor_tiles, tile_row, tile_col, right_sides, diag_inverse):
    levels = factor_tiles.shape[0]
    rows_dev = right_sides.shape[1]
    block = right_sides.shape[2]
    group_rows = rows_dev * n_row
    row_axis, col_axis = ("row", n_row), ("col", n_col)

    plan = [(None, row_axis)]
    plan += [(col_axis, row_axis)] * (levels - 1)
    plan += [(col_axis, col_axis)]
    plan += [(row_axis, col_axis)] * (levels - 1)
    plan += [(row_axis, None)]

    piece = right_sides.shape[1:]
    n_tiles = factor_tiles.shape[1]
    vmem = pl.BlockSpec(memory_space=pltpu.VMEM)
    smem = pl.BlockSpec(memory_space=pltpu.SMEM)
    scratch = [
        pltpu.VMEM((n_tiles,) + piece[1:], jnp.float32),
        pltpu.VMEM((n_tiles,) + piece[1:], jnp.float32),
        pltpu.SMEM((levels, n_col * rows_dev), jnp.int32),
        pltpu.SMEM((levels, n_col * rows_dev), jnp.int32),
        pltpu.SMEM((levels, group_rows), jnp.int32),
        pltpu.SMEM((levels, group_rows), jnp.int32),
    ]
    for ex, ga in plan:
        if ex:
            scratch += [
                pltpu.VMEM((ex[1],) + piece, jnp.bfloat16),
                pltpu.SemaphoreType.DMA((rows_dev, ex[1])),
                pltpu.SemaphoreType.DMA((rows_dev, ex[1])),
            ]
        if ga:
            targets = n_col if ga[0] == "row" else n_row
            scratch += [
                pltpu.VMEM((ga[1] * rows_dev,) + piece[1:], jnp.bfloat16),
                pltpu.VMEM(piece, jnp.bfloat16),
                pltpu.SemaphoreType.DMA((rows_dev, ga[1])),
                pltpu.SemaphoreType.DMA((rows_dev, ga[1])),
                pltpu.VMEM((targets,) + piece, jnp.bfloat16),
            ]
    args = [right_sides, diag_inverse, factor_tiles, tile_row, tile_col]
    specs = [vmem] * 3 + [smem] * 2
    return pl.pallas_call(
        functools.partial(solve_kernel, plan),
        out_shape=jax.ShapeDtypeStruct(right_sides.shape, jnp.float32),
        in_specs=specs,
        out_specs=vmem,
        scratch_shapes=scratch,
        compiler_params=pltpu.CompilerParams(collective_id=1, has_side_effects=True),
    )(*args)


def solution(mesh):
    n_row, n_col = mesh.shape["row"], mesh.shape["col"]
    return jax.shard_map(
        functools.partial(solve_all, n_row, n_col),
        mesh=mesh,
        in_specs=(
            P(None, "row", None, "col"),
            P(None, "row", "col"),
            P(None, "row", "col"),
            P(None, ("col", "row"), None, None),
            P(None, None, ("col", "row")),
        ),
        out_specs=P(None, ("col", "row"), None, None),
        check_vma=False,
    )
```

```python
import functools

import jax
import jax.numpy as jnp
from jax import lax
from jax.experimental import pallas as pl
from jax.experimental.pallas import tpu as pltpu
from jax.sharding import PartitionSpec as P

MESH = pl.DeviceIdType.MESH
AXES = ("row", "col")
HIGHEST = lax.Precision.HIGHEST


def offsets(n):
    out = []
    for d in range(1, n // 2 + 1):
        out += [d] if 2 * d == n else [d, n - d]
    return out


def peer_id(axis, peer):
    return tuple(peer if name == axis else lax.axis_index(name) for name in AXES)


def phase(cfg, base, gs, out, x, ids, tiles, keys, bufs, tiles_transposed=False, meanwhile=None):
    ex, ga = cfg
    blocks = base.shape[0]

    def exchange_copies(kb):
        axis, n = ex
        held_x, ex_send, ex_recv = bufs["ex"]
        me = lax.axis_index(axis)
        copies = []
        for k, d in enumerate(offsets(n), start=1):
            peer = lax.rem(me + d, n)
            copy = pltpu.make_async_remote_copy(
                src_ref=x.at[peer, kb],
                dst_ref=held_x.at[k, kb],
                send_sem=ex_send.at[kb, k],
                recv_sem=ex_recv.at[kb, k],
                device_id=peer_id(axis, peer),
                device_id_type=MESH,
            )
            copy.start()
            copies.append(copy)
        return copies

    gather_copies = []
    pending = exchange_copies(0) if ex else None
    for kb in range(blocks):
        value = base[kb]
        if ex:
            axis, n = ex
            held_x = bufs["ex"][0]
            me = lax.axis_index(axis)
            copies = pending
            if kb + 1 < blocks:
                for copy in copies:
                    copy.wait_send()
                pending = exchange_copies(kb + 1)
            total = x[me, kb].astype(jnp.float32)
            for k in range(1, n):
                copies[k - 1].wait_recv()
                total = total + held_x[k, kb].astype(jnp.float32)
            if kb + 1 == blocks:
                for copy in copies:
                    copy.wait_send()
            value = value - total
        width = value.shape[0]
        for diag, transposed in gs:
            d = diag[:, pl.ds(kb * width, width)]
            contract = 0 if transposed else 1
            value = lax.dot_general(d, value, (((contract,), (0,)), ((), ())),
                                    precision=HIGHEST, preferred_element_type=jnp.float32)
        out[kb] = value
        if ga:
            axis, n = ga
            held_g, stage, ga_send, ga_recv, _ = bufs["ga"]
            me = lax.axis_index(axis)
            stage[kb] = value.astype(stage.dtype)
            for k, d in enumerate(offsets(n), start=1):
                peer = lax.rem(me + d, n)
                copy = pltpu.make_async_remote_copy(
                    src_ref=stage.at[kb],
                    dst_ref=held_g.at[me * blocks + kb],
                    send_sem=ga_send.at[kb, k],
                    recv_sem=ga_recv.at[kb, k],
                    device_id=peer_id(axis, peer),
                    device_id_type=MESH,
                )
                copy.start()
                gather_copies.append(copy)
            held_g[me * blocks + kb] = value.astype(held_g.dtype)
    if not ga:
        return
    held_g, _, _, _, terms = bufs["ga"]
    prod, group = bufs["work"]
    if meanwhile is not None:
        meanwhile()
    for copy in gather_copies:
        copy.wait()
    n_tiles = prod.shape[0]

    def product(t, carry):
        contract = 0 if tiles_transposed else 1
        prod[t] = lax.dot_general(tiles[t], held_g[ids[t]], (((contract,), (0,)), ((), ())),
                                  preferred_element_type=jnp.float32)
        return carry

    lax.fori_loop(0, n_tiles, product, 0)
    key, first, has = keys

    def grouping(t, carry):
        mine = key[t]
        acc = jnp.zeros(prod.shape[1:], jnp.float32)
        for other in range(n_tiles):
            acc = acc + jnp.where(key[other] == mine, prod[other], 0.0)
        group[t] = acc
        return carry

    lax.fori_loop(0, n_tiles, grouping, 0)

    def place(q, carry):
        terms[q // blocks, q % blocks] = jnp.where(has[q] != 0, group[first[q]], 0.0).astype(terms.dtype)
        return carry

    lax.fori_loop(0, terms.shape[0] * blocks, place, 0)


def fill_tables(key, first, has):
    n_tiles = key.shape[1]
    for s in range(key.shape[0]):

        def body(q, carry, s=s):
            found = jnp.int32(0)
            hit_any = jnp.int32(0)
            for t in reversed(range(n_tiles)):
                hit = key[s, t] == q
                found = jnp.where(hit, jnp.int32(t), found)
                hit_any = jnp.where(hit, jnp.int32(1), hit_any)
            first[s, q] = found
            has[s, q] = hit_any
            return carry

        lax.fori_loop(0, first.shape[1], body, 0)


def solve_kernel(plan, *refs):
    refs = list(refs)
    (rhs, diag, tiles, row_ids, col_ids, out, prod, group,
     fwd_first, fwd_has, bwd_first, bwd_has) = [refs.pop(0) for _ in range(12)]
    bufs = []
    for ex, ga in plan:
        entry = {"work": (prod, group)}
        if ex:
            entry["ex"] = tuple(refs.pop(0) for _ in range(3))
        if ga:
            entry["ga"] = tuple(refs.pop(0) for _ in range(5))
        bufs.append(entry)

    peers = {}
    for ex, ga in plan:
        for group_axis in (ex, ga):
            if group_axis:
                peers[group_axis[0]] = group_axis[1]
    barrier = pltpu.get_barrier_semaphore()
    for axis, n in peers.items():
        me = lax.axis_index(axis)
        for k in range(1, n):
            pl.semaphore_signal(
                barrier, inc=1, device_id=peer_id(axis, lax.rem(me + k, n)), device_id_type=MESH
            )
    pl.semaphore_wait(barrier, sum(n - 1 for n in peers.values()))

    levels = tiles.shape[0]

    def tables():
        fill_tables(row_ids, fwd_first, fwd_has)
        fill_tables(col_ids, bwd_first, bwd_has)

    def fwd_keys(s):
        return row_ids.at[s], fwd_first.at[s], fwd_has.at[s]

    def bwd_keys(s):
        return col_ids.at[s], bwd_first.at[s], bwd_has.at[s]

    previous = None
    for p, cfg in enumerate(plan):
        x = previous
        if p < levels:
            phase(cfg, rhs.at[p], [(diag.at[p], True)], out.at[p], x, col_ids.at[p], tiles.at[p],
                  fwd_keys(p), bufs[p], meanwhile=tables if p == 0 else None)
        elif p == levels:
            phase(cfg, rhs.at[p], [(diag.at[p], True), (diag.at[p], False)], out.at[p], x,
                  row_ids.at[p - 1], tiles.at[p - 1], bwd_keys(p - 1), bufs[p], tiles_transposed=True)
        else:
            s = 2 * levels - p
            if s > 0:
                phase(cfg, out.at[s], [(diag.at[s], False)], out.at[s], x, row_ids.at[s - 1],
                      tiles.at[s - 1], bwd_keys(s - 1), bufs[p], tiles_transposed=True)
            else:
                phase(cfg, out.at[s], [(diag.at[s], False)], out.at[s], x, None, None, None, bufs[p])
        if cfg[1]:
            previous = bufs[p]["ga"][4]


def solve_all(n_row, n_col, factor_tiles, tile_row, tile_col, right_sides, diag_inverse):
    levels = factor_tiles.shape[0]
    rows_dev = right_sides.shape[1]
    block = right_sides.shape[2]
    group_rows = rows_dev * n_row
    row_axis, col_axis = ("row", n_row), ("col", n_col)

    plan = [(None, row_axis)]
    plan += [(col_axis, row_axis)] * (levels - 1)
    plan += [(col_axis, col_axis)]
    plan += [(row_axis, col_axis)] * (levels - 1)
    plan += [(row_axis, None)]

    piece = right_sides.shape[1:]
    n_tiles = factor_tiles.shape[1]
    vmem = pl.BlockSpec(memory_space=pltpu.VMEM)
    smem = pl.BlockSpec(memory_space=pltpu.SMEM)
    scratch = [
        pltpu.VMEM((n_tiles,) + piece[1:], jnp.float32),
        pltpu.VMEM((n_tiles,) + piece[1:], jnp.float32),
        pltpu.SMEM((levels, n_col * rows_dev), jnp.int32),
        pltpu.SMEM((levels, n_col * rows_dev), jnp.int32),
        pltpu.SMEM((levels, group_rows), jnp.int32),
        pltpu.SMEM((levels, group_rows), jnp.int32),
    ]
    for ex, ga in plan:
        if ex:
            scratch += [
                pltpu.VMEM((ex[1],) + piece, jnp.bfloat16),
                pltpu.SemaphoreType.DMA((rows_dev, ex[1])),
                pltpu.SemaphoreType.DMA((rows_dev, ex[1])),
            ]
        if ga:
            targets = n_col if ga[0] == "row" else n_row
            scratch += [
                pltpu.VMEM((ga[1] * rows_dev,) + piece[1:], jnp.bfloat16),
                pltpu.VMEM(piece, jnp.bfloat16),
                pltpu.SemaphoreType.DMA((rows_dev, ga[1])),
                pltpu.SemaphoreType.DMA((rows_dev, ga[1])),
                pltpu.VMEM((targets,) + piece, jnp.bfloat16),
            ]
    ids = [tile_row.reshape(tile_row.shape[:2]), tile_col.reshape(tile_col.shape[:2])]
    args = [right_sides, diag_inverse, factor_tiles] + ids
    specs = [vmem] * 3 + [smem] * 2
    return pl.pallas_call(
        functools.partial(solve_kernel, plan),
        out_shape=jax.ShapeDtypeStruct(right_sides.shape, jnp.float32),
        in_specs=specs,
        out_specs=vmem,
        scratch_shapes=scratch,
        compiler_params=pltpu.CompilerParams(collective_id=1, has_side_effects=True),
    )(*args)


def solution(mesh):
    n_row, n_col = mesh.shape["row"], mesh.shape["col"]
    return jax.shard_map(
        functools.partial(solve_all, n_row, n_col),
        mesh=mesh,
        in_specs=(
            P(None, "row", None, "col"),
            P(None, "row", "col"),
            P(None, "row", "col"),
            P(None, ("col", "row"), None, None),
            P(None, None, ("col", "row")),
        ),
        out_specs=P(None, ("col", "row"), None, None),
        check_vma=False,
    )
```

```python
import functools

import jax
import jax.numpy as jnp
from jax import lax
from jax.experimental import pallas as pl
from jax.experimental.pallas import tpu as pltpu
from jax.sharding import PartitionSpec as P

MESH = pl.DeviceIdType.MESH
AXES = ("row", "col")
HIGHEST = lax.Precision.HIGHEST


def peer_id(axis, peer):
    return tuple(peer if name == axis else lax.axis_index(name) for name in AXES)


def phase(cfg, base, gs, out, x, ids, tiles, keys, bufs, tiles_transposed=False, meanwhile=None):
    ex, ga = cfg
    blocks = base.shape[0]

    def exchange_copies(kb):
        axis, n = ex
        held_x, ex_send, ex_recv = bufs["ex"]
        me = lax.axis_index(axis)
        copies = []
        for k, d in enumerate(range(1, n), start=1):
            peer = lax.rem(me + d, n)
            copy = pltpu.make_async_remote_copy(
                src_ref=x.at[peer, kb],
                dst_ref=held_x.at[k, kb],
                send_sem=ex_send.at[kb, k],
                recv_sem=ex_recv.at[kb, k],
                device_id=peer_id(axis, peer),
                device_id_type=MESH,
            )
            copy.start()
            copies.append(copy)
        return copies

    gather_copies = []
    pending = exchange_copies(0) if ex else None
    for kb in range(blocks):
        value = base[kb]
        if ex:
            axis, n = ex
            held_x = bufs["ex"][0]
            me = lax.axis_index(axis)
            copies = pending
            if kb + 1 < blocks:
                for copy in copies:
                    copy.wait_send()
                pending = exchange_copies(kb + 1)
            total = x[me, kb].astype(jnp.float32)
            for k in range(1, n):
                copies[k - 1].wait_recv()
                total = total + held_x[k, kb].astype(jnp.float32)
            if kb + 1 == blocks:
                for copy in copies:
                    copy.wait_send()
            value = value - total
        width = value.shape[0]
        for diag, transposed in gs:
            d = diag[:, pl.ds(kb * width, width)]
            contract = 0 if transposed else 1
            value = lax.dot_general(d, value, (((contract,), (0,)), ((), ())),
                                    precision=HIGHEST, preferred_element_type=jnp.float32)
        out[kb] = value
        if ga:
            axis, n = ga
            held_g, stage, ga_send, ga_recv, _ = bufs["ga"]
            me = lax.axis_index(axis)
            stage[kb] = value.astype(stage.dtype)
            for k, d in enumerate(range(1, n), start=1):
                peer = lax.rem(me + d, n)
                copy = pltpu.make_async_remote_copy(
                    src_ref=stage.at[kb],
                    dst_ref=held_g.at[me * blocks + kb],
                    send_sem=ga_send.at[kb, k],
                    recv_sem=ga_recv.at[kb, k],
                    device_id=peer_id(axis, peer),
                    device_id_type=MESH,
                )
                copy.start()
                gather_copies.append(copy)
            held_g[me * blocks + kb] = value.astype(held_g.dtype)
    if not ga:
        return
    held_g, _, _, _, terms = bufs["ga"]
    prod, group = bufs["work"]
    if meanwhile is not None:
        meanwhile()
    for copy in gather_copies:
        copy.wait()
    n_tiles = prod.shape[0]

    def product(t, carry):
        contract = 0 if tiles_transposed else 1
        prod[t] = lax.dot_general(tiles[t], held_g[ids[t]], (((contract,), (0,)), ((), ())),
                                  preferred_element_type=jnp.float32)
        return carry

    lax.fori_loop(0, n_tiles, product, 0)
    key, first, has = keys

    def grouping(t, carry):
        mine = key[t]
        acc = jnp.zeros(prod.shape[1:], jnp.float32)
        for other in range(n_tiles):
            acc = acc + jnp.where(key[other] == mine, prod[other], 0.0)
        group[t] = acc
        return carry

    lax.fori_loop(0, n_tiles, grouping, 0)

    def place(q, carry):
        terms[q // blocks, q % blocks] = jnp.where(has[q] != 0, group[first[q]], 0.0).astype(terms.dtype)
        return carry

    lax.fori_loop(0, terms.shape[0] * blocks, place, 0)


def fill_tables(key, first, has):
    n_tiles = key.shape[1]
    for s in range(key.shape[0]):

        def body(q, carry, s=s):
            found = jnp.int32(0)
            hit_any = jnp.int32(0)
            for t in reversed(range(n_tiles)):
                hit = key[s, t] == q
                found = jnp.where(hit, jnp.int32(t), found)
                hit_any = jnp.where(hit, jnp.int32(1), hit_any)
            first[s, q] = found
            has[s, q] = hit_any
            return carry

        lax.fori_loop(0, first.shape[1], body, 0)


def solve_kernel(plan, *refs):
    refs = list(refs)
    (rhs, diag, tiles, row_ids, col_ids, out, prod, group,
     fwd_first, fwd_has, bwd_first, bwd_has) = [refs.pop(0) for _ in range(12)]
    bufs = []
    for ex, ga in plan:
        entry = {"work": (prod, group)}
        if ex:
            entry["ex"] = tuple(refs.pop(0) for _ in range(3))
        if ga:
            entry["ga"] = tuple(refs.pop(0) for _ in range(5))
        bufs.append(entry)

    peers = {}
    for ex, ga in plan:
        for group_axis in (ex, ga):
            if group_axis:
                peers[group_axis[0]] = group_axis[1]
    barrier = pltpu.get_barrier_semaphore()
    for axis, n in peers.items():
        me = lax.axis_index(axis)
        for k in range(1, n):
            pl.semaphore_signal(
                barrier, inc=1, device_id=peer_id(axis, lax.rem(me + k, n)), device_id_type=MESH
            )
    pl.semaphore_wait(barrier, sum(n - 1 for n in peers.values()))

    levels = tiles.shape[0]

    def tables():
        fill_tables(row_ids, fwd_first, fwd_has)
        fill_tables(col_ids, bwd_first, bwd_has)

    def fwd_keys(s):
        return row_ids.at[s], fwd_first.at[s], fwd_has.at[s]

    def bwd_keys(s):
        return col_ids.at[s], bwd_first.at[s], bwd_has.at[s]

    previous = None
    for p, cfg in enumerate(plan):
        x = previous
        if p < levels:
            phase(cfg, rhs.at[p], [(diag.at[p], True)], out.at[p], x, col_ids.at[p], tiles.at[p],
                  fwd_keys(p), bufs[p], meanwhile=tables if p == 0 else None)
        elif p == levels:
            phase(cfg, rhs.at[p], [(diag.at[p], True), (diag.at[p], False)], out.at[p], x,
                  row_ids.at[p - 1], tiles.at[p - 1], bwd_keys(p - 1), bufs[p], tiles_transposed=True)
        else:
            s = 2 * levels - p
            if s > 0:
                phase(cfg, out.at[s], [(diag.at[s], False)], out.at[s], x, row_ids.at[s - 1],
                      tiles.at[s - 1], bwd_keys(s - 1), bufs[p], tiles_transposed=True)
            else:
                phase(cfg, out.at[s], [(diag.at[s], False)], out.at[s], x, None, None, None, bufs[p])
        if cfg[1]:
            previous = bufs[p]["ga"][4]


def solve_all(n_row, n_col, factor_tiles, tile_row, tile_col, right_sides, diag_inverse):
    levels = factor_tiles.shape[0]
    rows_dev = right_sides.shape[1]
    block = right_sides.shape[2]
    group_rows = rows_dev * n_row
    row_axis, col_axis = ("row", n_row), ("col", n_col)

    plan = [(None, row_axis)]
    plan += [(col_axis, row_axis)] * (levels - 1)
    plan += [(col_axis, col_axis)]
    plan += [(row_axis, col_axis)] * (levels - 1)
    plan += [(row_axis, None)]

    piece = right_sides.shape[1:]
    n_tiles = factor_tiles.shape[1]
    vmem = pl.BlockSpec(memory_space=pltpu.VMEM)
    smem = pl.BlockSpec(memory_space=pltpu.SMEM)
    scratch = [
        pltpu.VMEM((n_tiles,) + piece[1:], jnp.float32),
        pltpu.VMEM((n_tiles,) + piece[1:], jnp.float32),
        pltpu.SMEM((levels, n_col * rows_dev), jnp.int32),
        pltpu.SMEM((levels, n_col * rows_dev), jnp.int32),
        pltpu.SMEM((levels, group_rows), jnp.int32),
        pltpu.SMEM((levels, group_rows), jnp.int32),
    ]
    for ex, ga in plan:
        if ex:
            scratch += [
                pltpu.VMEM((ex[1],) + piece, jnp.bfloat16),
                pltpu.SemaphoreType.DMA((rows_dev, ex[1])),
                pltpu.SemaphoreType.DMA((rows_dev, ex[1])),
            ]
        if ga:
            targets = n_col if ga[0] == "row" else n_row
            scratch += [
                pltpu.VMEM((ga[1] * rows_dev,) + piece[1:], jnp.bfloat16),
                pltpu.VMEM(piece, jnp.bfloat16),
                pltpu.SemaphoreType.DMA((rows_dev, ga[1])),
                pltpu.SemaphoreType.DMA((rows_dev, ga[1])),
                pltpu.VMEM((targets,) + piece, jnp.bfloat16),
            ]
    ids = [tile_row.reshape(tile_row.shape[:2]), tile_col.reshape(tile_col.shape[:2])]
    args = [right_sides, diag_inverse, factor_tiles] + ids
    specs = [vmem] * 3 + [smem] * 2
    return pl.pallas_call(
        functools.partial(solve_kernel, plan),
        out_shape=jax.ShapeDtypeStruct(right_sides.shape, jnp.float32),
        in_specs=specs,
        out_specs=vmem,
        scratch_shapes=scratch,
        compiler_params=pltpu.CompilerParams(collective_id=1, has_side_effects=True),
    )(*args)


def solution(mesh):
    n_row, n_col = mesh.shape["row"], mesh.shape["col"]
    return jax.shard_map(
        functools.partial(solve_all, n_row, n_col),
        mesh=mesh,
        in_specs=(
            P(None, "row", None, "col"),
            P(None, "row", "col"),
            P(None, "row", "col"),
            P(None, ("col", "row"), None, None),
            P(None, None, ("col", "row")),
        ),
        out_specs=P(None, ("col", "row"), None, None),
        check_vma=False,
    )
```

```python
import functools

import jax
import jax.numpy as jnp
from jax import lax
from jax.experimental import pallas as pl
from jax.experimental.pallas import tpu as pltpu
from jax.sharding import PartitionSpec as P

MESH = pl.DeviceIdType.MESH
AXES = ("row", "col")
HIGHEST = lax.Precision.HIGHEST


def peer_id(axis, peer):
    return tuple(peer if name == axis else lax.axis_index(name) for name in AXES)


def phase(cfg, base, gs, out, x, ids, tiles, keys, bufs, tiles_transposed=False, meanwhile=None):
    ex, ga = cfg
    blocks = base.shape[0]

    def exchange_copies(kb):
        axis, n = ex
        held_x, ex_send, ex_recv = bufs["ex"]
        me = lax.axis_index(axis)
        copies = []
        for k, d in enumerate(range(1, n), start=1):
            peer = lax.rem(me + d, n)
            copy = pltpu.make_async_remote_copy(
                src_ref=x.at[peer, kb],
                dst_ref=held_x.at[k, kb],
                send_sem=ex_send.at[kb, k],
                recv_sem=ex_recv.at[kb, k],
                device_id=peer_id(axis, peer),
                device_id_type=MESH,
            )
            copy.start()
            copies.append(copy)
        return copies

    gather_copies = []
    pending = exchange_copies(0) if ex else None
    for kb in range(blocks):
        value = base[kb]
        if ex:
            axis, n = ex
            held_x = bufs["ex"][0]
            me = lax.axis_index(axis)
            copies = pending
            if kb + 1 < blocks:
                for copy in copies:
                    copy.wait_send()
                pending = exchange_copies(kb + 1)
            total = x[me, kb].astype(jnp.float32)
            for k in range(1, n):
                copies[k - 1].wait_recv()
                total = total + held_x[k, kb].astype(jnp.float32)
            if kb + 1 == blocks:
                for copy in copies:
                    copy.wait_send()
            value = value - total
        width = value.shape[0]
        for diag, transposed in gs:
            d = diag[:, pl.ds(kb * width, width)]
            contract = 0 if transposed else 1
            value = lax.dot_general(d, value, (((contract,), (0,)), ((), ())),
                                    precision=HIGHEST, preferred_element_type=jnp.float32)
        out[kb] = value
        if ga:
            axis, n = ga
            held_g, stage, ga_send, ga_recv, _ = bufs["ga"]
            me = lax.axis_index(axis)
            stage[kb] = value.astype(stage.dtype)
            for k, d in enumerate(range(1, n), start=1):
                peer = lax.rem(me + d, n)
                copy = pltpu.make_async_remote_copy(
                    src_ref=stage.at[kb],
                    dst_ref=held_g.at[me * blocks + kb],
                    send_sem=ga_send.at[kb, k],
                    recv_sem=ga_recv.at[kb, k],
                    device_id=peer_id(axis, peer),
                    device_id_type=MESH,
                )
                copy.start()
                gather_copies.append(copy)
            held_g[me * blocks + kb] = value.astype(held_g.dtype)
    if not ga:
        return
    held_g, _, _, _, terms = bufs["ga"]
    prod, group = bufs["work"]
    if meanwhile is not None:
        meanwhile()
    for copy in gather_copies:
        copy.wait()
    n_tiles = prod.shape[0]

    def product(t, carry):
        contract = 0 if tiles_transposed else 1
        prod[t] = lax.dot_general(tiles[t], held_g[ids[t]], (((contract,), (0,)), ((), ())),
                                  preferred_element_type=jnp.float32)
        return carry

    lax.fori_loop(0, n_tiles, product, 0)
    key, first, has = keys

    def grouping(t, carry):
        mine = key[t]
        acc = jnp.zeros(prod.shape[1:], jnp.float32)
        for other in range(n_tiles):
            acc = acc + jnp.where(key[other] == mine, prod[other], 0.0)
        group[t] = acc
        return carry

    lax.fori_loop(0, n_tiles, grouping, 0)

    def place(q, carry):
        terms[q // blocks, q % blocks] = jnp.where(has[q] != 0, group[first[q]], 0.0).astype(terms.dtype)
        return carry

    lax.fori_loop(0, terms.shape[0] * blocks, place, 0)


def fill_tables(key, first, has):
    n_tiles = key.shape[1]
    for s in range(key.shape[0]):

        def body(q, carry, s=s):
            found = jnp.int32(0)
            hit_any = jnp.int32(0)
            for t in reversed(range(n_tiles)):
                hit = key[s, t] == q
                found = jnp.where(hit, jnp.int32(t), found)
                hit_any = jnp.where(hit, jnp.int32(1), hit_any)
            first[s, q] = found
            has[s, q] = hit_any
            return carry

        lax.fori_loop(0, first.shape[1], body, 0)


def solve_kernel(plan, *refs):
    refs = list(refs)
    (rhs, diag, tiles, row_ids, col_ids, out, prod, group,
     fwd_first, fwd_has, bwd_first, bwd_has, tiles_t) = [refs.pop(0) for _ in range(13)]
    bufs = []
    for ex, ga in plan:
        entry = {"work": (prod, group)}
        if ex:
            entry["ex"] = tuple(refs.pop(0) for _ in range(3))
        if ga:
            entry["ga"] = tuple(refs.pop(0) for _ in range(5))
        bufs.append(entry)

    peers = {}
    for ex, ga in plan:
        for group_axis in (ex, ga):
            if group_axis:
                peers[group_axis[0]] = group_axis[1]
    barrier = pltpu.get_barrier_semaphore()
    for axis, n in peers.items():
        me = lax.axis_index(axis)
        for k in range(1, n):
            pl.semaphore_signal(
                barrier, inc=1, device_id=peer_id(axis, lax.rem(me + k, n)), device_id_type=MESH
            )
    pl.semaphore_wait(barrier, sum(n - 1 for n in peers.values()))

    levels = tiles.shape[0]

    def tables():
        fill_tables(row_ids, fwd_first, fwd_has)
        fill_tables(col_ids, bwd_first, bwd_has)
        for s in range(levels):
            for t in range(tiles.shape[1]):
                tiles_t[s, t] = tiles[s, t].T

    def fwd_keys(s):
        return row_ids.at[s], fwd_first.at[s], fwd_has.at[s]

    def bwd_keys(s):
        return col_ids.at[s], bwd_first.at[s], bwd_has.at[s]

    previous = None
    for p, cfg in enumerate(plan):
        x = previous
        if p < levels:
            phase(cfg, rhs.at[p], [(diag.at[p], True)], out.at[p], x, col_ids.at[p], tiles.at[p],
                  fwd_keys(p), bufs[p], meanwhile=tables if p == 0 else None)
        elif p == levels:
            phase(cfg, rhs.at[p], [(diag.at[p], True), (diag.at[p], False)], out.at[p], x,
                  row_ids.at[p - 1], tiles_t.at[p - 1], bwd_keys(p - 1), bufs[p])
        else:
            s = 2 * levels - p
            if s > 0:
                phase(cfg, out.at[s], [(diag.at[s], False)], out.at[s], x, row_ids.at[s - 1],
                      tiles_t.at[s - 1], bwd_keys(s - 1), bufs[p])
            else:
                phase(cfg, out.at[s], [(diag.at[s], False)], out.at[s], x, None, None, None, bufs[p])
        if cfg[1]:
            previous = bufs[p]["ga"][4]


def solve_all(n_row, n_col, factor_tiles, tile_row, tile_col, right_sides, diag_inverse):
    levels = factor_tiles.shape[0]
    rows_dev = right_sides.shape[1]
    block = right_sides.shape[2]
    group_rows = rows_dev * n_row
    row_axis, col_axis = ("row", n_row), ("col", n_col)

    plan = [(None, row_axis)]
    plan += [(col_axis, row_axis)] * (levels - 1)
    plan += [(col_axis, col_axis)]
    plan += [(row_axis, col_axis)] * (levels - 1)
    plan += [(row_axis, None)]

    piece = right_sides.shape[1:]
    n_tiles = factor_tiles.shape[1]
    vmem = pl.BlockSpec(memory_space=pltpu.VMEM)
    smem = pl.BlockSpec(memory_space=pltpu.SMEM)
    scratch = [
        pltpu.VMEM((n_tiles,) + piece[1:], jnp.float32),
        pltpu.VMEM((n_tiles,) + piece[1:], jnp.float32),
        pltpu.SMEM((levels, n_col * rows_dev), jnp.int32),
        pltpu.SMEM((levels, n_col * rows_dev), jnp.int32),
        pltpu.SMEM((levels, group_rows), jnp.int32),
        pltpu.SMEM((levels, group_rows), jnp.int32),
        pltpu.VMEM(factor_tiles.shape, factor_tiles.dtype),
    ]
    for ex, ga in plan:
        if ex:
            scratch += [
                pltpu.VMEM((ex[1],) + piece, jnp.bfloat16),
                pltpu.SemaphoreType.DMA((rows_dev, ex[1])),
                pltpu.SemaphoreType.DMA((rows_dev, ex[1])),
            ]
        if ga:
            targets = n_col if ga[0] == "row" else n_row
            scratch += [
                pltpu.VMEM((ga[1] * rows_dev,) + piece[1:], jnp.bfloat16),
                pltpu.VMEM(piece, jnp.bfloat16),
                pltpu.SemaphoreType.DMA((rows_dev, ga[1])),
                pltpu.SemaphoreType.DMA((rows_dev, ga[1])),
                pltpu.VMEM((targets,) + piece, jnp.bfloat16),
            ]
    ids = [tile_row.reshape(tile_row.shape[:2]), tile_col.reshape(tile_col.shape[:2])]
    args = [right_sides, diag_inverse, factor_tiles] + ids
    specs = [vmem] * 3 + [smem] * 2
    return pl.pallas_call(
        functools.partial(solve_kernel, plan),
        out_shape=jax.ShapeDtypeStruct(right_sides.shape, jnp.float32),
        in_specs=specs,
        out_specs=vmem,
        scratch_shapes=scratch,
        compiler_params=pltpu.CompilerParams(collective_id=1, has_side_effects=True),
    )(*args)


def solution(mesh):
    n_row, n_col = mesh.shape["row"], mesh.shape["col"]
    return jax.shard_map(
        functools.partial(solve_all, n_row, n_col),
        mesh=mesh,
        in_specs=(
            P(None, "row", None, "col"),
            P(None, "row", "col"),
            P(None, "row", "col"),
            P(None, ("col", "row"), None, None),
            P(None, None, ("col", "row")),
        ),
        out_specs=P(None, ("col", "row"), None, None),
        check_vma=False,
    )
```

```python
import functools

import jax
import jax.numpy as jnp
from jax import lax
from jax.experimental import pallas as pl
from jax.experimental.pallas import tpu as pltpu
from jax.sharding import PartitionSpec as P

MESH = pl.DeviceIdType.MESH
AXES = ("row", "col")
HIGHEST = lax.Precision.HIGHEST


def peer_id(axis, peer):
    return tuple(peer if name == axis else lax.axis_index(name) for name in AXES)


def phase(cfg, base, gs, out, x, ids, tiles, keys, bufs, tiles_transposed=False, meanwhile=None):
    ex, ga = cfg
    blocks = base.shape[0]

    def exchange_copies(kb):
        axis, n = ex
        held_x, ex_send, ex_recv = bufs["ex"]
        me = lax.axis_index(axis)
        copies = []
        for k, d in enumerate(range(1, n), start=1):
            peer = lax.rem(me + d, n)
            copy = pltpu.make_async_remote_copy(
                src_ref=x.at[peer, kb],
                dst_ref=held_x.at[k, kb],
                send_sem=ex_send.at[kb, k],
                recv_sem=ex_recv.at[kb, k],
                device_id=peer_id(axis, peer),
                device_id_type=MESH,
            )
            copy.start()
            copies.append(copy)
        return copies

    gather_copies = []
    pending = exchange_copies(0) if ex else None
    for kb in range(blocks):
        value = base[kb]
        if ex:
            axis, n = ex
            held_x = bufs["ex"][0]
            me = lax.axis_index(axis)
            copies = pending
            if kb + 1 < blocks:
                for copy in copies:
                    copy.wait_send()
                pending = exchange_copies(kb + 1)
            total = x[me, kb].astype(jnp.float32)
            for k in range(1, n):
                copies[k - 1].wait_recv()
                total = total + held_x[k, kb].astype(jnp.float32)
            if kb + 1 == blocks:
                for copy in copies:
                    copy.wait_send()
            value = value - total
        width = value.shape[0]
        for diag, transposed in gs:
            if transposed is None:
                d, contract = diag[kb], 1
            else:
                d = diag[:, pl.ds(kb * width, width)]
                contract = 0 if transposed else 1
            value = lax.dot_general(d, value, (((contract,), (0,)), ((), ())),
                                    precision=HIGHEST, preferred_element_type=jnp.float32)
        out[kb] = value
        if ga:
            axis, n = ga
            held_g, stage, ga_send, ga_recv, _ = bufs["ga"]
            me = lax.axis_index(axis)
            stage[kb] = value.astype(stage.dtype)
            for k, d in enumerate(range(1, n), start=1):
                peer = lax.rem(me + d, n)
                copy = pltpu.make_async_remote_copy(
                    src_ref=stage.at[kb],
                    dst_ref=held_g.at[me * blocks + kb],
                    send_sem=ga_send.at[kb, k],
                    recv_sem=ga_recv.at[kb, k],
                    device_id=peer_id(axis, peer),
                    device_id_type=MESH,
                )
                copy.start()
                gather_copies.append(copy)
            held_g[me * blocks + kb] = value.astype(held_g.dtype)
    if not ga:
        return
    held_g, _, _, _, terms = bufs["ga"]
    prod, group = bufs["work"]
    if meanwhile is not None:
        meanwhile()
    for copy in gather_copies:
        copy.wait()
    n_tiles = prod.shape[0]

    def product(t, carry):
        contract = 0 if tiles_transposed else 1
        prod[t] = lax.dot_general(tiles[t], held_g[ids[t]], (((contract,), (0,)), ((), ())),
                                  preferred_element_type=jnp.float32)
        return carry

    lax.fori_loop(0, n_tiles, product, 0)
    key, first, has = keys

    def grouping(t, carry):
        mine = key[t]
        acc = jnp.zeros(prod.shape[1:], jnp.float32)
        for other in range(n_tiles):
            acc = acc + jnp.where(key[other] == mine, prod[other], 0.0)
        group[t] = acc
        return carry

    lax.fori_loop(0, n_tiles, grouping, 0)

    def place(q, carry):
        terms[q // blocks, q % blocks] = jnp.where(has[q] != 0, group[first[q]], 0.0).astype(terms.dtype)
        return carry

    lax.fori_loop(0, terms.shape[0] * blocks, place, 0)


def fill_tables(key, first, has):
    n_tiles = key.shape[1]
    for s in range(key.shape[0]):

        def body(q, carry, s=s):
            found = jnp.int32(0)
            hit_any = jnp.int32(0)
            for t in reversed(range(n_tiles)):
                hit = key[s, t] == q
                found = jnp.where(hit, jnp.int32(t), found)
                hit_any = jnp.where(hit, jnp.int32(1), hit_any)
            first[s, q] = found
            has[s, q] = hit_any
            return carry

        lax.fori_loop(0, first.shape[1], body, 0)


def solve_kernel(plan, *refs):
    refs = list(refs)
    (rhs, diag, tiles, row_ids, col_ids, out, prod, group,
     fwd_first, fwd_has, bwd_first, bwd_has, tiles_t, g_fwd) = [refs.pop(0) for _ in range(14)]
    bufs = []
    for ex, ga in plan:
        entry = {"work": (prod, group)}
        if ex:
            entry["ex"] = tuple(refs.pop(0) for _ in range(3))
        if ga:
            entry["ga"] = tuple(refs.pop(0) for _ in range(5))
        bufs.append(entry)

    peers = {}
    for ex, ga in plan:
        for group_axis in (ex, ga):
            if group_axis:
                peers[group_axis[0]] = group_axis[1]
    barrier = pltpu.get_barrier_semaphore()
    for axis, n in peers.items():
        me = lax.axis_index(axis)
        for k in range(1, n):
            pl.semaphore_signal(
                barrier, inc=1, device_id=peer_id(axis, lax.rem(me + k, n)), device_id_type=MESH
            )
    pl.semaphore_wait(barrier, sum(n - 1 for n in peers.values()))

    levels = tiles.shape[0]

    def tables():
        fill_tables(row_ids, fwd_first, fwd_has)
        fill_tables(col_ids, bwd_first, bwd_has)
        for s in range(levels):
            for t in range(tiles.shape[1]):
                tiles_t[s, t] = tiles[s, t].T
        width = g_fwd.shape[-1]
        for s in range(1, levels + 1):
            for kb in range(g_fwd.shape[1]):
                g_fwd[s, kb] = diag[s, :, pl.ds(kb * width, width)].T

    def fwd_keys(s):
        return row_ids.at[s], fwd_first.at[s], fwd_has.at[s]

    def bwd_keys(s):
        return col_ids.at[s], bwd_first.at[s], bwd_has.at[s]

    previous = None
    for p, cfg in enumerate(plan):
        x = previous
        if p < levels:
            g = (diag.at[p], True) if p == 0 else (g_fwd.at[p], None)
            phase(cfg, rhs.at[p], [g], out.at[p], x, col_ids.at[p], tiles.at[p],
                  fwd_keys(p), bufs[p], meanwhile=tables if p == 0 else None)
        elif p == levels:
            phase(cfg, rhs.at[p], [(g_fwd.at[p], None), (diag.at[p], False)], out.at[p], x,
                  row_ids.at[p - 1], tiles_t.at[p - 1], bwd_keys(p - 1), bufs[p])
        else:
            s = 2 * levels - p
            if s > 0:
                phase(cfg, out.at[s], [(diag.at[s], False)], out.at[s], x, row_ids.at[s - 1],
                      tiles_t.at[s - 1], bwd_keys(s - 1), bufs[p])
            else:
                phase(cfg, out.at[s], [(diag.at[s], False)], out.at[s], x, None, None, None, bufs[p])
        if cfg[1]:
            previous = bufs[p]["ga"][4]


def solve_all(n_row, n_col, factor_tiles, tile_row, tile_col, right_sides, diag_inverse):
    levels = factor_tiles.shape[0]
    rows_dev = right_sides.shape[1]
    block = right_sides.shape[2]
    group_rows = rows_dev * n_row
    row_axis, col_axis = ("row", n_row), ("col", n_col)

    plan = [(None, row_axis)]
    plan += [(col_axis, row_axis)] * (levels - 1)
    plan += [(col_axis, col_axis)]
    plan += [(row_axis, col_axis)] * (levels - 1)
    plan += [(row_axis, None)]

    piece = right_sides.shape[1:]
    n_tiles = factor_tiles.shape[1]
    vmem = pl.BlockSpec(memory_space=pltpu.VMEM)
    smem = pl.BlockSpec(memory_space=pltpu.SMEM)
    scratch = [
        pltpu.VMEM((n_tiles,) + piece[1:], jnp.float32),
        pltpu.VMEM((n_tiles,) + piece[1:], jnp.float32),
        pltpu.SMEM((levels, n_col * rows_dev), jnp.int32),
        pltpu.SMEM((levels, n_col * rows_dev), jnp.int32),
        pltpu.SMEM((levels, group_rows), jnp.int32),
        pltpu.SMEM((levels, group_rows), jnp.int32),
        pltpu.VMEM(factor_tiles.shape, factor_tiles.dtype),
        pltpu.VMEM((levels + 1, rows_dev, block, block), jnp.float32),
    ]
    for ex, ga in plan:
        if ex:
            scratch += [
                pltpu.VMEM((ex[1],) + piece, jnp.bfloat16),
                pltpu.SemaphoreType.DMA((rows_dev, ex[1])),
                pltpu.SemaphoreType.DMA((rows_dev, ex[1])),
            ]
        if ga:
            targets = n_col if ga[0] == "row" else n_row
            scratch += [
                pltpu.VMEM((ga[1] * rows_dev,) + piece[1:], jnp.bfloat16),
                pltpu.VMEM(piece, jnp.bfloat16),
                pltpu.SemaphoreType.DMA((rows_dev, ga[1])),
                pltpu.SemaphoreType.DMA((rows_dev, ga[1])),
                pltpu.VMEM((targets,) + piece, jnp.bfloat16),
            ]
    ids = [tile_row.reshape(tile_row.shape[:2]), tile_col.reshape(tile_col.shape[:2])]
    args = [right_sides, diag_inverse, factor_tiles] + ids
    specs = [vmem] * 3 + [smem] * 2
    return pl.pallas_call(
        functools.partial(solve_kernel, plan),
        out_shape=jax.ShapeDtypeStruct(right_sides.shape, jnp.float32),
        in_specs=specs,
        out_specs=vmem,
        scratch_shapes=scratch,
        compiler_params=pltpu.CompilerParams(collective_id=1, has_side_effects=True),
    )(*args)


def solution(mesh):
    n_row, n_col = mesh.shape["row"], mesh.shape["col"]
    return jax.shard_map(
        functools.partial(solve_all, n_row, n_col),
        mesh=mesh,
        in_specs=(
            P(None, "row", None, "col"),
            P(None, "row", "col"),
            P(None, "row", "col"),
            P(None, ("col", "row"), None, None),
            P(None, None, ("col", "row")),
        ),
        out_specs=P(None, ("col", "row"), None, None),
        check_vma=False,
    )
```

```python
import functools

import jax
import jax.numpy as jnp
from jax import lax
from jax.experimental import pallas as pl
from jax.experimental.pallas import tpu as pltpu
from jax.sharding import PartitionSpec as P

MESH = pl.DeviceIdType.MESH
AXES = ("row", "col")
HIGHEST = lax.Precision.HIGHEST


def peer_id(axis, peer):
    return tuple(peer if name == axis else lax.axis_index(name) for name in AXES)


def phase(cfg, base, gs, out, x, ids, tiles, keys, bufs, tiles_transposed=False, meanwhile=None):
    ex, ga = cfg
    blocks = base.shape[0]

    def exchange_copies(kb):
        axis, n = ex
        held_x, ex_send, ex_recv = bufs["ex"]
        me = lax.axis_index(axis)
        copies = []
        for k, d in enumerate(range(1, n), start=1):
            peer = lax.rem(me + d, n)
            copy = pltpu.make_async_remote_copy(
                src_ref=x.at[peer, kb],
                dst_ref=held_x.at[k, kb],
                send_sem=ex_send.at[kb, k],
                recv_sem=ex_recv.at[kb, k],
                device_id=peer_id(axis, peer),
                device_id_type=MESH,
            )
            copy.start()
            copies.append(copy)
        return copies

    gather_copies = []
    pending = exchange_copies(0) if ex else None
    for kb in range(blocks):
        value = base[kb]
        if ex:
            axis, n = ex
            held_x = bufs["ex"][0]
            me = lax.axis_index(axis)
            copies = pending
            if kb + 1 < blocks:
                for copy in copies:
                    copy.wait_send()
                pending = exchange_copies(kb + 1)
            total = x[me, kb].astype(jnp.float32)
            for k in range(1, n):
                copies[k - 1].wait_recv()
                total = total + held_x[k, kb].astype(jnp.float32)
            if kb + 1 == blocks:
                for copy in copies:
                    copy.wait_send()
            value = value - total
        width = value.shape[0]
        for diag, transposed in gs:
            if transposed is None:
                d, contract = diag[kb], 1
            else:
                d = diag[:, pl.ds(kb * width, width)]
                contract = 0 if transposed else 1
            value = lax.dot_general(d, value, (((contract,), (0,)), ((), ())),
                                    precision=HIGHEST, preferred_element_type=jnp.float32)
        out[kb] = value
        if ga:
            axis, n = ga
            held_g, stage, ga_send, ga_recv, _ = bufs["ga"]
            me = lax.axis_index(axis)
            stage[kb] = value.astype(stage.dtype)
            for k, d in enumerate(range(1, n), start=1):
                peer = lax.rem(me + d, n)
                copy = pltpu.make_async_remote_copy(
                    src_ref=stage.at[kb],
                    dst_ref=held_g.at[me * blocks + kb],
                    send_sem=ga_send.at[kb, k],
                    recv_sem=ga_recv.at[kb, k],
                    device_id=peer_id(axis, peer),
                    device_id_type=MESH,
                )
                copy.start()
                gather_copies.append(copy)
            held_g[me * blocks + kb] = value.astype(held_g.dtype)
    if not ga:
        return
    held_g, _, _, _, terms = bufs["ga"]
    prod, group = bufs["work"]
    if meanwhile is not None:
        meanwhile()
    for copy in gather_copies:
        copy.wait()
    n_tiles = prod.shape[0]

    def product(t, carry):
        contract = 0 if tiles_transposed else 1
        prod[t] = lax.dot_general(tiles[t], held_g[ids[t]], (((contract,), (0,)), ((), ())),
                                  preferred_element_type=jnp.float32)
        return carry

    lax.fori_loop(0, n_tiles, product, 0, unroll=True)
    key, first, has = keys

    def grouping(t, carry):
        mine = key[t]
        acc = jnp.zeros(prod.shape[1:], jnp.float32)
        for other in range(n_tiles):
            acc = acc + jnp.where(key[other] == mine, prod[other], 0.0)
        group[t] = acc
        return carry

    lax.fori_loop(0, n_tiles, grouping, 0, unroll=True)

    def place(q, carry):
        terms[q // blocks, q % blocks] = jnp.where(has[q] != 0, group[first[q]], 0.0).astype(terms.dtype)
        return carry

    lax.fori_loop(0, terms.shape[0] * blocks, place, 0)


def fill_tables(key, first, has):
    n_tiles = key.shape[1]
    for s in range(key.shape[0]):

        def body(q, carry, s=s):
            found = jnp.int32(0)
            hit_any = jnp.int32(0)
            for t in reversed(range(n_tiles)):
                hit = key[s, t] == q
                found = jnp.where(hit, jnp.int32(t), found)
                hit_any = jnp.where(hit, jnp.int32(1), hit_any)
            first[s, q] = found
            has[s, q] = hit_any
            return carry

        lax.fori_loop(0, first.shape[1], body, 0)


def solve_kernel(plan, *refs):
    refs = list(refs)
    (rhs, diag, tiles, row_ids, col_ids, out, prod, group,
     fwd_first, fwd_has, bwd_first, bwd_has, tiles_t, g_fwd) = [refs.pop(0) for _ in range(14)]
    bufs = []
    for ex, ga in plan:
        entry = {"work": (prod, group)}
        if ex:
            entry["ex"] = tuple(refs.pop(0) for _ in range(3))
        if ga:
            entry["ga"] = tuple(refs.pop(0) for _ in range(5))
        bufs.append(entry)

    peers = {}
    for ex, ga in plan:
        for group_axis in (ex, ga):
            if group_axis:
                peers[group_axis[0]] = group_axis[1]
    barrier = pltpu.get_barrier_semaphore()
    for axis, n in peers.items():
        me = lax.axis_index(axis)
        for k in range(1, n):
            pl.semaphore_signal(
                barrier, inc=1, device_id=peer_id(axis, lax.rem(me + k, n)), device_id_type=MESH
            )
    pl.semaphore_wait(barrier, sum(n - 1 for n in peers.values()))

    levels = tiles.shape[0]

    def tables():
        fill_tables(row_ids, fwd_first, fwd_has)
        fill_tables(col_ids, bwd_first, bwd_has)
        for s in range(levels):
            for t in range(tiles.shape[1]):
                tiles_t[s, t] = tiles[s, t].T
        width = g_fwd.shape[-1]
        for s in range(1, levels + 1):
            for kb in range(g_fwd.shape[1]):
                g_fwd[s, kb] = diag[s, :, pl.ds(kb * width, width)].T

    def fwd_keys(s):
        return row_ids.at[s], fwd_first.at[s], fwd_has.at[s]

    def bwd_keys(s):
        return col_ids.at[s], bwd_first.at[s], bwd_has.at[s]

    previous = None
    for p, cfg in enumerate(plan):
        x = previous
        if p < levels:
            g = (diag.at[p], True) if p == 0 else (g_fwd.at[p], None)
            phase(cfg, rhs.at[p], [g], out.at[p], x, col_ids.at[p], tiles.at[p],
                  fwd_keys(p), bufs[p], meanwhile=tables if p == 0 else None)
        elif p == levels:
            phase(cfg, rhs.at[p], [(g_fwd.at[p], None), (diag.at[p], False)], out.at[p], x,
                  row_ids.at[p - 1], tiles_t.at[p - 1], bwd_keys(p - 1), bufs[p])
        else:
            s = 2 * levels - p
            if s > 0:
                phase(cfg, out.at[s], [(diag.at[s], False)], out.at[s], x, row_ids.at[s - 1],
                      tiles_t.at[s - 1], bwd_keys(s - 1), bufs[p])
            else:
                phase(cfg, out.at[s], [(diag.at[s], False)], out.at[s], x, None, None, None, bufs[p])
        if cfg[1]:
            previous = bufs[p]["ga"][4]


def solve_all(n_row, n_col, factor_tiles, tile_row, tile_col, right_sides, diag_inverse):
    levels = factor_tiles.shape[0]
    rows_dev = right_sides.shape[1]
    block = right_sides.shape[2]
    group_rows = rows_dev * n_row
    row_axis, col_axis = ("row", n_row), ("col", n_col)

    plan = [(None, row_axis)]
    plan += [(col_axis, row_axis)] * (levels - 1)
    plan += [(col_axis, col_axis)]
    plan += [(row_axis, col_axis)] * (levels - 1)
    plan += [(row_axis, None)]

    piece = right_sides.shape[1:]
    n_tiles = factor_tiles.shape[1]
    vmem = pl.BlockSpec(memory_space=pltpu.VMEM)
    smem = pl.BlockSpec(memory_space=pltpu.SMEM)
    scratch = [
        pltpu.VMEM((n_tiles,) + piece[1:], jnp.float32),
        pltpu.VMEM((n_tiles,) + piece[1:], jnp.float32),
        pltpu.SMEM((levels, n_col * rows_dev), jnp.int32),
        pltpu.SMEM((levels, n_col * rows_dev), jnp.int32),
        pltpu.SMEM((levels, group_rows), jnp.int32),
        pltpu.SMEM((levels, group_rows), jnp.int32),
        pltpu.VMEM(factor_tiles.shape, factor_tiles.dtype),
        pltpu.VMEM((levels + 1, rows_dev, block, block), jnp.float32),
    ]
    for ex, ga in plan:
        if ex:
            scratch += [
                pltpu.VMEM((ex[1],) + piece, jnp.bfloat16),
                pltpu.SemaphoreType.DMA((rows_dev, ex[1])),
                pltpu.SemaphoreType.DMA((rows_dev, ex[1])),
            ]
        if ga:
            targets = n_col if ga[0] == "row" else n_row
            scratch += [
                pltpu.VMEM((ga[1] * rows_dev,) + piece[1:], jnp.bfloat16),
                pltpu.VMEM(piece, jnp.bfloat16),
                pltpu.SemaphoreType.DMA((rows_dev, ga[1])),
                pltpu.SemaphoreType.DMA((rows_dev, ga[1])),
                pltpu.VMEM((targets,) + piece, jnp.bfloat16),
            ]
    ids = [tile_row.reshape(tile_row.shape[:2]), tile_col.reshape(tile_col.shape[:2])]
    args = [right_sides, diag_inverse, factor_tiles] + ids
    specs = [vmem] * 3 + [smem] * 2
    return pl.pallas_call(
        functools.partial(solve_kernel, plan),
        out_shape=jax.ShapeDtypeStruct(right_sides.shape, jnp.float32),
        in_specs=specs,
        out_specs=vmem,
        scratch_shapes=scratch,
        compiler_params=pltpu.CompilerParams(collective_id=1, has_side_effects=True),
    )(*args)


def solution(mesh):
    n_row, n_col = mesh.shape["row"], mesh.shape["col"]
    return jax.shard_map(
        functools.partial(solve_all, n_row, n_col),
        mesh=mesh,
        in_specs=(
            P(None, "row", None, "col"),
            P(None, "row", "col"),
            P(None, "row", "col"),
            P(None, ("col", "row"), None, None),
            P(None, None, ("col", "row")),
        ),
        out_specs=P(None, ("col", "row"), None, None),
        check_vma=False,
    )
```

```python
import functools

import jax
import jax.numpy as jnp
from jax import lax
from jax.experimental import pallas as pl
from jax.experimental.pallas import tpu as pltpu
from jax.sharding import PartitionSpec as P

MESH = pl.DeviceIdType.MESH
AXES = ("row", "col")
HIGHEST = lax.Precision.HIGHEST


def peer_id(axis, peer):
    return tuple(peer if name == axis else lax.axis_index(name) for name in AXES)


def phase(cfg, base, gs, out, x, ids, tiles, keys, bufs, tiles_transposed=False, meanwhile=None):
    ex, ga = cfg
    blocks = base.shape[0]

    def exchange_copies(kb):
        axis, n = ex
        held_x, ex_send, ex_recv = bufs["ex"]
        me = lax.axis_index(axis)
        copies = []
        for k, d in enumerate(range(1, n), start=1):
            peer = lax.rem(me + d, n)
            copy = pltpu.make_async_remote_copy(
                src_ref=x.at[peer, kb],
                dst_ref=held_x.at[k, kb],
                send_sem=ex_send.at[kb, k],
                recv_sem=ex_recv.at[kb, k],
                device_id=peer_id(axis, peer),
                device_id_type=MESH,
            )
            copy.start()
            copies.append(copy)
        return copies

    gather_copies = []
    pending = exchange_copies(0) if ex else None
    for kb in range(blocks):
        value = base[kb]
        if ex:
            axis, n = ex
            held_x = bufs["ex"][0]
            me = lax.axis_index(axis)
            copies = pending
            if kb + 1 < blocks:
                for copy in copies:
                    copy.wait_send()
                pending = exchange_copies(kb + 1)
            total = x[me, kb].astype(jnp.float32)
            for k in range(1, n):
                copies[k - 1].wait_recv()
                total = total + held_x[k, kb].astype(jnp.float32)
            if kb + 1 == blocks:
                for copy in copies:
                    copy.wait_send()
            value = value - total
        width = value.shape[0]
        for diag, transposed in gs:
            if transposed is None:
                d, contract = diag[kb], 1
            else:
                d = diag[:, pl.ds(kb * width, width)]
                contract = 0 if transposed else 1
            value = lax.dot_general(d, value, (((contract,), (0,)), ((), ())),
                                    precision=HIGHEST, preferred_element_type=jnp.float32)
        out[kb] = value
        if ga:
            axis, n = ga
            held_g, stage, ga_send, ga_recv, _ = bufs["ga"]
            me = lax.axis_index(axis)
            stage[kb] = value.astype(stage.dtype)
            for k, d in enumerate(range(1, n), start=1):
                peer = lax.rem(me + d, n)
                copy = pltpu.make_async_remote_copy(
                    src_ref=stage.at[kb],
                    dst_ref=held_g.at[me * blocks + kb],
                    send_sem=ga_send.at[kb, k],
                    recv_sem=ga_recv.at[kb, k],
                    device_id=peer_id(axis, peer),
                    device_id_type=MESH,
                )
                copy.start()
                gather_copies.append(copy)
            held_g[me * blocks + kb] = value.astype(held_g.dtype)
    if not ga:
        return
    held_g, _, _, _, terms = bufs["ga"]
    prod, group = bufs["work"]
    if meanwhile is not None:
        meanwhile()
    for copy in gather_copies:
        copy.wait()
    n_tiles = prod.shape[0]

    def product(t, carry):
        contract = 0 if tiles_transposed else 1
        prod[t] = lax.dot_general(tiles[t], held_g[ids[t]], (((contract,), (0,)), ((), ())),
                                  preferred_element_type=jnp.float32)
        return carry

    lax.fori_loop(0, n_tiles, product, 0, unroll=True)
    key, first, has = keys

    def grouping(t, carry):
        mine = key[t]
        acc = jnp.zeros(prod.shape[1:], jnp.float32)
        for other in range(n_tiles):
            acc = acc + jnp.where(key[other] == mine, prod[other], 0.0)
        group[t] = acc
        return carry

    lax.fori_loop(0, n_tiles, grouping, 0, unroll=True)

    def place(q, carry):
        terms[q // blocks, q % blocks] = jnp.where(has[q] != 0, group[first[q]], 0.0).astype(terms.dtype)
        return carry

    lax.fori_loop(0, terms.shape[0] * blocks, place, 0, unroll=True)


def fill_tables(key, first, has):
    n_tiles = key.shape[1]
    for s in range(key.shape[0]):

        def body(q, carry, s=s):
            found = jnp.int32(0)
            hit_any = jnp.int32(0)
            for t in reversed(range(n_tiles)):
                hit = key[s, t] == q
                found = jnp.where(hit, jnp.int32(t), found)
                hit_any = jnp.where(hit, jnp.int32(1), hit_any)
            first[s, q] = found
            has[s, q] = hit_any
            return carry

        lax.fori_loop(0, first.shape[1], body, 0)


def solve_kernel(plan, *refs):
    refs = list(refs)
    (rhs, diag, tiles, row_ids, col_ids, out, prod, group,
     fwd_first, fwd_has, bwd_first, bwd_has, tiles_t, g_fwd) = [refs.pop(0) for _ in range(14)]
    bufs = []
    for ex, ga in plan:
        entry = {"work": (prod, group)}
        if ex:
            entry["ex"] = tuple(refs.pop(0) for _ in range(3))
        if ga:
            entry["ga"] = tuple(refs.pop(0) for _ in range(5))
        bufs.append(entry)

    peers = {}
    for ex, ga in plan:
        for group_axis in (ex, ga):
            if group_axis:
                peers[group_axis[0]] = group_axis[1]
    barrier = pltpu.get_barrier_semaphore()
    for axis, n in peers.items():
        me = lax.axis_index(axis)
        for k in range(1, n):
            pl.semaphore_signal(
                barrier, inc=1, device_id=peer_id(axis, lax.rem(me + k, n)), device_id_type=MESH
            )
    pl.semaphore_wait(barrier, sum(n - 1 for n in peers.values()))

    levels = tiles.shape[0]

    def tables():
        fill_tables(row_ids, fwd_first, fwd_has)
        fill_tables(col_ids, bwd_first, bwd_has)
        for s in range(levels):
            for t in range(tiles.shape[1]):
                tiles_t[s, t] = tiles[s, t].T
        width = g_fwd.shape[-1]
        for s in range(1, levels + 1):
            for kb in range(g_fwd.shape[1]):
                g_fwd[s, kb] = diag[s, :, pl.ds(kb * width, width)].T

    def fwd_keys(s):
        return row_ids.at[s], fwd_first.at[s], fwd_has.at[s]

    def bwd_keys(s):
        return col_ids.at[s], bwd_first.at[s], bwd_has.at[s]

    previous = None
    for p, cfg in enumerate(plan):
        x = previous
        if p < levels:
            g = (diag.at[p], True) if p == 0 else (g_fwd.at[p], None)
            phase(cfg, rhs.at[p], [g], out.at[p], x, col_ids.at[p], tiles.at[p],
                  fwd_keys(p), bufs[p], meanwhile=tables if p == 0 else None)
        elif p == levels:
            phase(cfg, rhs.at[p], [(g_fwd.at[p], None), (diag.at[p], False)], out.at[p], x,
                  row_ids.at[p - 1], tiles_t.at[p - 1], bwd_keys(p - 1), bufs[p])
        else:
            s = 2 * levels - p
            if s > 0:
                phase(cfg, out.at[s], [(diag.at[s], False)], out.at[s], x, row_ids.at[s - 1],
                      tiles_t.at[s - 1], bwd_keys(s - 1), bufs[p])
            else:
                phase(cfg, out.at[s], [(diag.at[s], False)], out.at[s], x, None, None, None, bufs[p])
        if cfg[1]:
            previous = bufs[p]["ga"][4]


def solve_all(n_row, n_col, factor_tiles, tile_row, tile_col, right_sides, diag_inverse):
    levels = factor_tiles.shape[0]
    rows_dev = right_sides.shape[1]
    block = right_sides.shape[2]
    group_rows = rows_dev * n_row
    row_axis, col_axis = ("row", n_row), ("col", n_col)

    plan = [(None, row_axis)]
    plan += [(col_axis, row_axis)] * (levels - 1)
    plan += [(col_axis, col_axis)]
    plan += [(row_axis, col_axis)] * (levels - 1)
    plan += [(row_axis, None)]

    piece = right_sides.shape[1:]
    n_tiles = factor_tiles.shape[1]
    vmem = pl.BlockSpec(memory_space=pltpu.VMEM)
    smem = pl.BlockSpec(memory_space=pltpu.SMEM)
    scratch = [
        pltpu.VMEM((n_tiles,) + piece[1:], jnp.float32),
        pltpu.VMEM((n_tiles,) + piece[1:], jnp.float32),
        pltpu.SMEM((levels, n_col * rows_dev), jnp.int32),
        pltpu.SMEM((levels, n_col * rows_dev), jnp.int32),
        pltpu.SMEM((levels, group_rows), jnp.int32),
        pltpu.SMEM((levels, group_rows), jnp.int32),
        pltpu.VMEM(factor_tiles.shape, factor_tiles.dtype),
        pltpu.VMEM((levels + 1, rows_dev, block, block), jnp.float32),
    ]
    for ex, ga in plan:
        if ex:
            scratch += [
                pltpu.VMEM((ex[1],) + piece, jnp.bfloat16),
                pltpu.SemaphoreType.DMA((rows_dev, ex[1])),
                pltpu.SemaphoreType.DMA((rows_dev, ex[1])),
            ]
        if ga:
            targets = n_col if ga[0] == "row" else n_row
            scratch += [
                pltpu.VMEM((ga[1] * rows_dev,) + piece[1:], jnp.bfloat16),
                pltpu.VMEM(piece, jnp.bfloat16),
                pltpu.SemaphoreType.DMA((rows_dev, ga[1])),
                pltpu.SemaphoreType.DMA((rows_dev, ga[1])),
                pltpu.VMEM((targets,) + piece, jnp.bfloat16),
            ]
    ids = [tile_row.reshape(tile_row.shape[:2]), tile_col.reshape(tile_col.shape[:2])]
    args = [right_sides, diag_inverse, factor_tiles] + ids
    specs = [vmem] * 3 + [smem] * 2
    return pl.pallas_call(
        functools.partial(solve_kernel, plan),
        out_shape=jax.ShapeDtypeStruct(right_sides.shape, jnp.float32),
        in_specs=specs,
        out_specs=vmem,
        scratch_shapes=scratch,
        compiler_params=pltpu.CompilerParams(collective_id=1, has_side_effects=True),
    )(*args)


def solution(mesh):
    n_row, n_col = mesh.shape["row"], mesh.shape["col"]
    return jax.shard_map(
        functools.partial(solve_all, n_row, n_col),
        mesh=mesh,
        in_specs=(
            P(None, "row", None, "col"),
            P(None, "row", "col"),
            P(None, "row", "col"),
            P(None, ("col", "row"), None, None),
            P(None, None, ("col", "row")),
        ),
        out_specs=P(None, ("col", "row"), None, None),
        check_vma=False,
    )
```
